512 devices in a mesh: section: 8 (over x, core), expert: 64 (over y, z).
Axes of the slice: x: 4, y: 8, z: 8, core: 2. Of those that a mesh axis runs over, the one named last changes fastest.
Arguments:
- activations: bfloat16 [8, 4096, 3584], P('section', 'expert'), may hold values from -6 to 6
- gradients: bfloat16 [8, 4096, 3584], P('section', 'expert'), may hold values from -6 to 6
- stashed: bfloat16 [2, 8, 4096, 3584], P(None, 'section', 'expert'), may hold values from -6 to 6
- fresh_activations: bfloat16 [1, 4096, 3584], P(None, 'expert'), may hold values from -6 to 6
- fresh_gradients: bfloat16 [1, 4096, 3584], P(None, 'expert'), may hold values from -6 to 6
- w_up: bfloat16 [8, 3584, 8192], P('section', None, 'expert'), may hold values from -0.09375 to 0.09375
- w_down: bfloat16 [8, 8192, 3584], P('section', 'expert'), may hold values from -0.125 to 0.125
- forward_routes: int32 [2, 8, 4096, 8], P(None, 'section', 'expert'), may hold values from 0 to 255, as said below
- forward_gates: float32 [2, 8, 4096, 8], P(None, 'section', 'expert'), may hold values from 0.25 to 2.5
- backward_routes: int32 [2, 8, 4096, 8], P(None, 'section', 'expert'), may hold values from 0 to 255, as said below
- backward_gates: float32 [2, 8, 4096, 8], P(None, 'section', 'expert'), may hold values from 0.25 to 2.5
Outputs:
- section_outputs: bfloat16 [8, 4096, 3584], P('section', 'expert')
- input_gradients: bfloat16 [8, 4096, 3584], P('section', 'expert')
The draws below stay inside these ranges and needn't reach their ends.
Inputs may be any that keep to these rules, and one draw needn't show every extreme that they name: `forward_routes`: the ids of one token are distinct. For every step and section, no id below 4 is named by more than 3 tokens of one device's block of 64 tokens, and some id below 4 is named by exactly 3 tokens of every device's block. `backward_routes`: the ids of one token are distinct. For every step and section, no id below 4 is named by more than 3 tokens of one device's block of 64 tokens, and some id below 4 is named by exactly 3 tokens of every device's block.
All inputs are finite; a program needn't handle non-finite values.
Results may differ from the reference program's by a relative error of at most 0.005.
Values may be sent and summed in bfloat16 or wider, within the bound.
A program may use at most 64 MiB of HBM per device.

```python
import jax
import jax.numpy as jnp
from jax import lax

D = 3584
HID = 2048
HID_DEV = 128
ROUTED = 256
TOP = 8
CAP = 3
TOK_DEV = 64
STEPS = 2
SECTIONS = 8
TOKENS = 4096
SLICES = 16
WINDOW = 4
COLS = 8192


def route_table(key):
    blocks = TOKENS // TOK_DEV
    shape = (STEPS, SECTIONS, blocks, TOK_DEV)
    keys = jax.random.split(key, 6)
    scores = jax.random.randint(keys[0], shape + (ROUTED,), 0, 1048576) * ROUTED + jnp.arange(ROUTED, dtype=jnp.int32)
    scores = jnp.where(jnp.arange(ROUTED, dtype=jnp.int32) < WINDOW, -1, scores)
    unused, chosen = lax.top_k(scores, TOP)
    counts = jax.random.randint(keys[1], (STEPS, SECTIONS, blocks, WINDOW), 0, CAP + 1)
    fullest = jax.random.randint(keys[2], (STEPS, SECTIONS, 1, 1), 0, WINDOW)
    counts = jnp.where(jnp.arange(WINDOW, dtype=jnp.int32) == fullest, CAP, counts)
    offsets = jax.random.randint(keys[3], (STEPS, SECTIONS, blocks, WINDOW), 0, TOK_DEV)
    turns = jax.random.randint(keys[4], shape, 0, TOP)
    order_scores = jax.random.randint(keys[5], shape, 0, 1048576) * TOK_DEV + jnp.arange(TOK_DEV, dtype=jnp.int32)
    positions = jnp.argsort(jnp.argsort(order_scores, axis=-1), axis=-1).astype(jnp.int32)
    spots_all = jnp.arange(TOP, dtype=jnp.int32)
    for member in range(WINDOW):
        struck = (positions - offsets[..., member:member + 1]) % TOK_DEV < counts[..., member:member + 1]
        target = (turns + member) % TOP
        placed = struck[..., None] & (spots_all == target[..., None])
        chosen = jnp.where(placed, member, chosen)
    return chosen.reshape(STEPS, SECTIONS, TOKENS, TOP).astype(jnp.int32)


def draw_forward_routes(key, part):
    return route_table(jax.random.fold_in(key, 11))


def draw_backward_routes(key, part):
    return route_table(jax.random.fold_in(key, 23))


def block_scale(stream_key, extent, cuts, least, top_value):
    def one(axis_at, blocks):
        steps = jax.random.uniform(jax.random.fold_in(jax.random.fold_in(stream_key, 6), axis_at), (blocks,), jnp.float32, least / len(cuts), top_value / len(cuts))
        return jnp.repeat(jnp.exp(steps), extent[axis_at] // blocks).reshape((-1,) + (1,) * (len(extent) - axis_at - 1))

    factor_of = one(*cuts[0])
    for cut in cuts[1:]:
        factor_of = factor_of * one(*cut)
    return factor_of


def centred(rng, dims, spread, reach, cuts=(), held_as=jnp.bfloat16):
    drawn = spread * jax.random.normal(rng, dims, jnp.float32)
    if cuts:
        drawn = drawn * block_scale(rng, dims, cuts, -0.22, 0.18)
    return jnp.clip(drawn, -reach, reach).astype(held_as)


def setup_inputs(seed: int = 0) -> dict:
    seeds = jax.random.split(jax.random.key(seed), 12)
    return {
        "activations": centred(seeds[0], (SECTIONS, TOKENS, D), 1.0, 6.0, ((0, 8), (1, 64))),
        "gradients": centred(seeds[1], (SECTIONS, TOKENS, D), 1.0, 6.0, ((0, 8), (1, 64))),
        "stashed": centred(seeds[2], (STEPS, SECTIONS, TOKENS, D), 1.0, 6.0, ((1, 8), (2, 64))),
        "fresh_activations": centred(seeds[3], (STEPS - 1, TOKENS, D), 1.0, 6.0, ((1, 64),)),
        "fresh_gradients": centred(seeds[4], (STEPS - 1, TOKENS, D), 1.0, 6.0, ((1, 64),)),
        "w_up": centred(seeds[5], (SECTIONS, D, COLS), D ** -0.5, 0.09375, ((0, 8), (2, 64))),
        "w_down": centred(seeds[6], (SECTIONS, COLS, D), HID ** -0.5, 0.125, ((0, 8), (1, 64))),
        "forward_routes": draw_forward_routes(jax.random.fold_in(seeds[11], 71), 0),
        "forward_gates": jnp.clip(0.25 + 2.25 * jax.random.uniform(seeds[8], (STEPS, SECTIONS, TOKENS, TOP), jnp.float32) ** block_scale(seeds[8], (STEPS, SECTIONS, TOKENS, TOP), ((1, 8), (2, 64)), -0.2, 0.2), 0.25, 2.5),
        "backward_routes": draw_backward_routes(jax.random.fold_in(seeds[11], 71), 0),
        "backward_gates": jnp.clip(0.25 + 2.25 * jax.random.uniform(seeds[10], (STEPS, SECTIONS, TOKENS, TOP), jnp.float32) ** block_scale(seeds[10], (STEPS, SECTIONS, TOKENS, TOP), ((1, 8), (2, 64)), -0.2, 0.2), 0.25, 2.5),
    }


def slot_plan(routes, gates):
    match = routes[:, :, None] == jnp.arange(WINDOW, dtype=jnp.int32)[None, None, :]
    chosen = jnp.sum(match.astype(jnp.float32), axis=1)
    weight = jnp.sum(jnp.where(match, gates[:, :, None], jnp.zeros_like(gates)[:, :, None]), axis=1)
    ranks = jnp.cumsum(chosen, axis=0) - chosen
    places = (ranks[:, :, None] == jnp.arange(CAP, dtype=jnp.float32)[None, None, :]).astype(jnp.float32)
    return places * chosen[:, :, None], weight


def expert_rows(places, tokens):
    picked = jnp.einsum('ntec,ntd->encd', places, tokens.astype(jnp.float32))
    return picked.astype(jnp.bfloat16)


def slice_sum(parts):
    rounded = lax.optimization_barrier(parts.astype(jnp.bfloat16))
    return jnp.sum(rounded.astype(jnp.float32), axis=1)


def spread_back(places, weight, totals, tokens):
    scaled = places * weight[:, :, :, None]
    mixed = jnp.einsum('ntec,encd->ntd', scaled, totals, precision=lax.Precision.HIGHEST)
    return (tokens.astype(jnp.float32) + mixed).astype(jnp.bfloat16)


def plan_blocks(routes, gates):
    blocks = TOKENS // TOK_DEV
    return jax.vmap(slot_plan)(routes.reshape(blocks, TOK_DEV, TOP), gates.reshape(blocks, TOK_DEV, TOP))


def section_forward(tokens, routes, gates, up_section, down_section):
    blocks = TOKENS // TOK_DEV
    token_blocks = tokens.reshape(blocks, TOK_DEV, D)
    places, weight = plan_blocks(routes, gates)
    rows = expert_rows(places, token_blocks)
    totals = []
    for member in range(WINDOW):
        picked = rows[member].reshape(blocks * CAP, D)
        up_block = up_section[:, member * HID:(member + 1) * HID]
        down_block = down_section[member * HID:(member + 1) * HID]
        pre = jnp.dot(picked, up_block, preferred_element_type=jnp.float32)
        hidden = jax.nn.silu(pre).astype(jnp.bfloat16)
        parts = jnp.einsum('rjh,jhd->rjd', hidden.reshape(blocks * CAP, SLICES, HID_DEV).astype(jnp.float32),
                           down_block.reshape(SLICES, HID_DEV, D).astype(jnp.float32))
        totals.append(slice_sum(parts).reshape(blocks, CAP, D))
    totals = jnp.stack(totals)
    return spread_back(places, weight, totals, token_blocks).reshape(TOKENS, D)


def section_backward(saved, arriving, routes, gates, up_section, down_section):
    blocks = TOKENS // TOK_DEV
    saved_blocks = saved.reshape(blocks, TOK_DEV, D)
    grad_blocks = arriving.reshape(blocks, TOK_DEV, D)
    places, weight = plan_blocks(routes, gates)
    rows_saved = expert_rows(places, saved_blocks)
    rows_grad = expert_rows(places, grad_blocks)
    totals = []
    for member in range(WINDOW):
        picked = rows_saved[member].reshape(blocks * CAP, D)
        picked_grad = rows_grad[member].reshape(blocks * CAP, D)
        up_block = up_section[:, member * HID:(member + 1) * HID]
        down_block = down_section[member * HID:(member + 1) * HID]
        pre = jnp.dot(picked, up_block, preferred_element_type=jnp.float32)
        sigma = jax.nn.sigmoid(pre)
        slope = sigma * (1.0 + pre * (1.0 - sigma))
        dhidden = jnp.dot(picked_grad, down_block.T, preferred_element_type=jnp.float32)
        dpre = (dhidden * slope).astype(jnp.bfloat16)
        parts = jnp.einsum('rjh,djh->rjd', dpre.reshape(blocks * CAP, SLICES, HID_DEV).astype(jnp.float32),
                           up_block.reshape(D, SLICES, HID_DEV).astype(jnp.float32))
        totals.append(slice_sum(parts).reshape(blocks, CAP, D))
    totals = jnp.stack(totals)
    return spread_back(places, weight, totals, grad_blocks).reshape(TOKENS, D)


def run_section(pieces):
    inputs, arriving, saved, route_ahead, gate_ahead, route_behind, gate_behind, up_section, down_section = pieces
    result = section_forward(inputs, route_ahead, gate_ahead, up_section, down_section)
    returned = section_backward(saved, arriving, route_behind, gate_behind, up_section, down_section)
    return result, returned


def reference(activations, gradients, stashed, fresh_activations, fresh_gradients, w_up, w_down,
              forward_routes, forward_gates, backward_routes, backward_gates):
    current = activations
    flowing = gradients
    outputs = activations
    returned = gradients
    for window_step in range(STEPS):
        outputs, returned = lax.map(run_section, (current, flowing, stashed[window_step],
                                                forward_routes[window_step], forward_gates[window_step],
                                                backward_routes[window_step], backward_gates[window_step],
                                                w_up, w_down))
        if window_step + 1 < STEPS:
            current = jnp.concatenate([fresh_activations[window_step][None], outputs[:-1]], axis=0)
            flowing = jnp.concatenate([returned[1:], fresh_gradients[window_step][None]], axis=0)
    return outputs, returned
```

```python
import jax
import jax.numpy as jnp
import numpy as np
from jax import lax
from jax.experimental import pallas as pl
from jax.experimental.pallas import tpu as pltpu
from jax.sharding import PartitionSpec as P

CAP = 3
STEPS = 2
WINDOW = 4
TOK = 64
D = 3584
W = D // 2
C = W // 2
HID_DEV = 128
NY = 8
NZ = 8
PAD = 16
ROWS = 3 * NY * CAP
BACK = 2 * NY * CAP
HALF = NY * CAP
BF = jnp.bfloat16
F32 = jnp.float32
TRANS = (((1,), (1,)), ((), ()))
FAR_FIRST = (4, 3, 5, 2, 6, 1, 7)


def dot(a, b):
    return jnp.dot(a, b, preferred_element_type=F32)


def dot_t(a, b):
    return lax.dot_general(a, b, TRANS, preferred_element_type=F32)


def kernel(x_in, g_in, st_in, fx_in, fg_in, up_in, dn_in, pk_in, sc_in, cmp_in, exp_in,
           out_ref, dx_ref,
           xs, gs, upf, dnf, upc, sendy, ybuf, zbuf, pp, xsend, xrecv, pbuf, ra, rb, rsend, ret,
           w_ss, w_rs, y_ss, y_rs, za_ss, za_rs, zb_ss, zb_rs, e_ss, e_rs,
           ra_ss, ra_rs, rb_ss, rb_rs, t_ss, t_rs, s_ss, s_rs):
    sec = lax.axis_index("section")
    me = lax.axis_index("expert")
    y = me // NZ
    z = me % NZ
    par = y % 2
    mate = (y + 1 - 2 * par) * NZ + z
    flip = sec % 2
    sgn = 1 - 2 * flip
    to_a = y * NZ + (z + sgn + NZ) % NZ
    to_b = y * NZ + (z - sgn + NZ) % NZ
    sec_up = (sec + 1) % 8
    sec_dn = (sec + 7) % 8

    def at(block):
        return (block + 2 * NZ) % NZ

    def remote(src, dst, ss, rs, expert, section=None):
        return pltpu.make_async_remote_copy(
            src_ref=src, dst_ref=dst, send_sem=ss, recv_sem=rs,
            device_id=(sec if section is None else section, expert),
            device_id_type=pl.DeviceIdType.MESH)

    barrier = pltpu.get_barrier_semaphore()
    peers = [(sec, ((y + k) % NY) * NZ + z) for k in range(1, NY)]
    peers += [(sec, to_a), (sec, to_b), (sec_up, me), (sec_dn, me)]
    for peer in peers:
        pl.semaphore_signal(barrier, inc=1, device_id=peer, device_id_type=pl.DeviceIdType.MESH)
    xs[0] = x_in[...]
    gs[0] = g_in[...]
    pl.semaphore_wait(barrier, len(peers))

    def weight_copies():
        return (
            remote(up_in.at[1 - par], upf.at[par], w_ss.at[0], w_rs.at[0], mate),
            remote(dn_in.at[1 - par], dnf.at[par], w_ss.at[1], w_rs.at[1], mate),
        )

    def step(t, carry):
        @pl.when(t == 1)
        def _():
            up_shift, dn_shift = shift_copies()
            up_shift.wait()
            dn_shift.wait()

            @pl.when(sec == 0)
            def _():
                xs[1] = fx_in[...]

            @pl.when(sec == 7)
            def _():
                gs[1] = fg_in[...]

        picked = dot(pk_in[t, 0], xs[t]) + dot(pk_in[t, 1], st_in[t]) + dot(pk_in[t, 2], gs[t])
        picked = picked.astype(BF)
        for e in range(WINDOW):
            for half in range(2):
                sendy[t, 2 * e + half] = picked[e * PAD:(e + 1) * PAD, half * W:(half + 1) * W]
        sent_y = []
        for k in FAR_FIRST:
            to = (y + k) % NY
            copy = remote(sendy.at[t, to], ybuf.at[t, y], y_ss.at[t, k], y_rs.at[t, k], to * NZ + z)
            copy.start()
            sent_y.append(copy)
        ybuf[t, y] = sendy[t, y]
        for copy in sent_y:
            copy.wait_recv()

        @pl.when(t == 0)
        def _():
            for copy in weight_copies():
                copy.start()

        block = dot(cmp_in[...], ybuf[t].reshape(NY * PAD, W)).astype(BF)
        for c in range(2):
            zbuf[t, z, c] = block[:, c * C:(c + 1) * C]

        def go_a(h, c):
            b = at(z - sgn * h)
            return remote(zbuf.at[t, b, c], zbuf.at[t, b, c], za_ss.at[t, h, c], za_rs.at[t, h, c], to_a)

        def go_b(h, c):
            b = at(z + sgn * h)
            return remote(zbuf.at[t, b, c], zbuf.at[t, b, c], zb_ss.at[t, h, c], zb_rs.at[t, h, c], to_b)

        def swap(b):
            return remote(xsend.at[t, b], xrecv.at[t, b], e_ss.at[t, b], e_rs.at[t, b], mate)

        def first_half(b):
            rows = [zbuf[t, b, c] for c in range(2)]
            pre = dot(rows[0][:BACK], upc[:C]) + dot(rows[1][:BACK], upc[C:])
            down = dnf[...].reshape(2 * HID_DEV, W)
            dh = dot_t(rows[0][BACK:], down[:, :C]) + dot_t(rows[1][BACK:], down[:, C:])
            both = jnp.concatenate([pre, dh], axis=0)
            pp[t, b] = both
            xsend[t, b] = both.astype(BF)
            swap(b).start()

        for c in range(2):
            go_a(0, c).start()
            go_b(0, c).start()
        for h in range(4):
            for c in range(2):
                go_a(h, c).wait_recv()
                if h < 3:
                    go_a(h + 1, c).start()
                    go_b(h, c).wait_recv()
                    if h < 2:
                        go_b(h + 1, c).start()
            if h == 1:
                @pl.when(t == 0)
                def _():
                    upf[par] = up_in[par]
                    dnf[par] = dn_in[par]
                    for copy in weight_copies():
                        copy.wait()
                    upc[:, :HID_DEV] = upf[0]
                    upc[:, HID_DEV:] = upf[1]

                first_half(z)
                first_half(at(z - sgn))
                first_half(at(z + sgn))
            if h >= 1:
                first_half(at(z - sgn * (h + 1)))
                if h < 3:
                    first_half(at(z + sgn * (h + 1)))

        def second_half(b):
            swap(b).wait_recv()
            both = pp[t, b] + xrecv[t, b].astype(F32)
            v = both[:HALF]
            hidden = (v / (1.0 + jnp.exp(-v))).astype(BF)
            u = both[HALF:BACK]
            sigma = 1.0 / (1.0 + jnp.exp(-u))
            dpre = (both[BACK:] * (sigma * (1.0 + u * (1.0 - sigma)))).astype(BF)
            part = dot(hidden, dnf[...].reshape(2 * HID_DEV, W))
            for c in range(2):
                dpart = dot_t(dpre, upc[c * C:(c + 1) * C])
                pbuf[t, b, c] = jnp.concatenate([part[:, c * C:(c + 1) * C], dpart], axis=0).astype(BF)

        def back_a(h, c):
            b = at(z + sgn * (4 - h))
            return remote(pbuf.at[t, b, c], ra.at[t, h, c], ra_ss.at[t, h, c], ra_rs.at[t, h, c], to_a)

        def back_b(h, c):
            b = at(z - sgn * (3 - h))
            return remote(pbuf.at[t, b, c], rb.at[t, h, c], rb_ss.at[t, h, c], rb_rs.at[t, h, c], to_b)

        for h in range(4):
            b = at(z + sgn * (4 - h))
            second_half(b)
            for c in range(2):
                if h > 0:
                    back_a(h - 1, c).wait_recv()
                    pbuf[t, b, c] = (pbuf[t, b, c].astype(F32) + ra[t, h - 1, c].astype(F32)).astype(BF)
                back_a(h, c).start()
            if h < 3:
                b = at(z - sgn * (3 - h))
                second_half(b)
                for c in range(2):
                    if h > 0:
                        back_b(h - 1, c).wait_recv()
                        pbuf[t, b, c] = (pbuf[t, b, c].astype(F32) + rb[t, h - 1, c].astype(F32)).astype(BF)
                    back_b(h, c).start()
        second_half(z)
        for c in range(2):
            back_b(2, c).wait_recv()
            back_a(3, c).wait_recv()
            total = (pbuf[t, z, c].astype(F32) + ra[t, 3, c].astype(F32) + rb[t, 2, c].astype(F32)).astype(BF)
            spread = dot(exp_in[...], total).astype(BF)
            for k in range(NY):
                rsend[t, k, :, c * C:(c + 1) * C] = spread[k * 8:(k + 1) * 8]
        sent_t = []
        for k in FAR_FIRST:
            to = (y + k) % NY
            copy = remote(rsend.at[t, to], ret.at[t, y], t_ss.at[t, k], t_rs.at[t, k], to * NZ + z)
            copy.start()
            sent_t.append(copy)
        ret[t, y] = rsend[t, y]
        for copy in sent_t:
            copy.wait_recv()
        for half in range(2):
            totals = jnp.concatenate([ret[t, 2 * e + half].astype(F32) for e in range(WINDOW)], axis=0)
            cols = slice(half * W, (half + 1) * W)
            for ref, own, which in ((out_ref, xs, 0), (dx_ref, gs, 1)):
                mixed = jnp.dot(sc_in[t, which], totals, precision=lax.Precision.HIGHEST,
                                preferred_element_type=F32)
                ref[:, cols] = (own[t, :, cols].astype(F32) + mixed).astype(BF)

        @pl.when(t == 0)
        def _():
            for copy in shift_copies():
                copy.start()

        for copy in sent_y + sent_t:
            copy.wait_send()
        for c in range(2):
            for h in range(4):
                go_a(h, c).wait_send()
                back_a(h, c).wait_send()
            for h in range(3):
                go_b(h, c).wait_send()
                back_b(h, c).wait_send()
        for b in range(NZ):
            swap(b).wait_send()
        return carry

    def shift_copies():
        return (
            remote(out_ref, xs.at[1], s_ss.at[0], s_rs.at[0], me, sec_up),
            remote(dx_ref, gs.at[1], s_ss.at[1], s_rs.at[1], me, sec_dn),
        )

    lax.fori_loop(0, STEPS, step, 0)


def slot_plan(routes, gates):
    match = routes[..., None] == jnp.arange(WINDOW, dtype=jnp.int32)
    chosen = jnp.sum(match.astype(F32), axis=2)
    weight = jnp.sum(jnp.where(match, gates[..., None], 0.0), axis=2)
    ranks = jnp.cumsum(chosen, axis=1) - chosen
    places = (ranks[..., None] == jnp.arange(CAP, dtype=F32)).astype(F32)
    return places * chosen[..., None], weight


def plans(fr, fg, br, bg):
    pf, wf = slot_plan(fr, fg)
    pb, wb = slot_plan(br, bg)

    def picker(places, s):
        m = jnp.transpose(places, (0, 2, 3, 1))
        m = jnp.pad(m, ((0, 0), (0, 0), (s * CAP, PAD - (s + 1) * CAP), (0, 0)))
        return m.reshape(STEPS, WINDOW * PAD, TOK).astype(BF)

    def scaler(places, weight, s):
        m = places * weight[..., None]
        m = jnp.pad(m, ((0, 0), (0, 0), (0, 0), (s * CAP, 8 - (s + 1) * CAP)))
        return m.reshape(STEPS, TOK, WINDOW * 8)

    pick = jnp.stack([picker(pf, 0), picker(pb, 1), picker(pb, 2)], axis=1)
    scale = jnp.stack([scaler(pf, wf, 0), scaler(pb, wb, 1)], axis=1)
    return pick, scale


def constants():
    i = np.arange(ROWS)
    j = np.arange(NY * PAD)
    s, k, c = i // HALF, (i % HALF) // CAP, i % CAP
    squeeze = ((k * PAD + s * CAP + c)[:, None] == j[None, :])
    i = np.arange(BACK)
    s, k, c = i // HALF, (i % HALF) // CAP, i % CAP
    spread = (np.arange(NY * 8)[:, None] == (k * 8 + s * CAP + c)[None, :])
    return jnp.asarray(squeeze, BF), jnp.asarray(spread, BF)


def local(activations, gradients, stashed, fresh_activations, fresh_gradients, w_up, w_down,
          forward_routes, forward_gates, backward_routes, backward_gates):
    pick, scale = plans(forward_routes[:, 0], forward_gates[:, 0], backward_routes[:, 0], backward_gates[:, 0])
    squeeze, spread = constants()
    up = w_up[0].reshape(2, W, HID_DEV)
    down = jnp.stack([w_down[0][:, :W], w_down[0][:, W:]])
    vmem = pl.BlockSpec(memory_space=pltpu.VMEM)
    dma = pltpu.SemaphoreType.DMA
    shape = jax.ShapeDtypeStruct((TOK, D), BF)
    S = STEPS
    out, dx = pl.pallas_call(
        kernel,
        out_shape=(shape, shape),
        in_specs=[vmem] * 11,
        out_specs=(vmem, vmem),
        scratch_shapes=[
            pltpu.VMEM((S, TOK, D), BF),
            pltpu.VMEM((S, TOK, D), BF),
            pltpu.VMEM((2, W, HID_DEV), BF),
            pltpu.VMEM((2, HID_DEV, W), BF),
            pltpu.VMEM((W, 2 * HID_DEV), BF),
            pltpu.VMEM((S, NY, PAD, W), BF),
            pltpu.VMEM((S, NY, PAD, W), BF),
            pltpu.VMEM((S, NZ, 2, ROWS, C), BF),
            pltpu.VMEM((S, NZ, ROWS, 2 * HID_DEV), F32),
            pltpu.VMEM((S, NZ, ROWS, 2 * HID_DEV), BF),
            pltpu.VMEM((S, NZ, ROWS, 2 * HID_DEV), BF),
            pltpu.VMEM((S, NZ, 2, BACK, C), BF),
            pltpu.VMEM((S, 4, 2, BACK, C), BF),
            pltpu.VMEM((S, 3, 2, BACK, C), BF),
            pltpu.VMEM((S, NY, 8, W), BF),
            pltpu.VMEM((S, NY, 8, W), BF),
            dma((2,)), dma((2,)),
            dma((S, NY)), dma((S, NY)),
            dma((S, 4, 2)), dma((S, 4, 2)),
            dma((S, 3, 2)), dma((S, 3, 2)),
            dma((S, NZ)), dma((S, NZ)),
            dma((S, 4, 2)), dma((S, 4, 2)),
            dma((S, 3, 2)), dma((S, 3, 2)),
            dma((S, NY)), dma((S, NY)),
            dma((2,)), dma((2,)),
        ],
        compiler_params=pltpu.CompilerParams(
            collective_id=0, has_side_effects=True, vmem_limit_bytes=60 * 1024 * 1024),
    )(activations[0], gradients[0], stashed[:, 0], fresh_activations[0], fresh_gradients[0],
      up, down, pick, scale, squeeze, spread)
    return out[None], dx[None]


def solution(mesh):
    placed = (
        P("section", "expert", None),
        P("section", "expert", None),
        P(None, "section", "expert", None),
        P(None, "expert", None),
        P(None, "expert", None),
        P("section", None, "expert"),
        P("section", "expert", None),
        P(None, "section", "expert", None),
        P(None, "section", "expert", None),
        P(None, "section", "expert", None),
        P(None, "section", "expert", None),
    )
    return jax.shard_map(
        local,
        mesh=mesh,
        in_specs=placed,
        out_specs=(P("section", "expert", None), P("section", "expert", None)),
        check_vma=False,
    )
```

```python
import jax
import jax.numpy as jnp
import numpy as np
from jax import lax
from jax.experimental import pallas as pl
from jax.experimental.pallas import tpu as pltpu
from jax.sharding import PartitionSpec as P

CAP = 3
STEPS = 2
WINDOW = 4
TOK = 64
D = 3584
W = D // 2
C = W // 2
HID_DEV = 128
NY = 8
NZ = 8
PAD = 16
ROWS = 3 * NY * CAP
BACK = 2 * NY * CAP
HALF = NY * CAP
BF = jnp.bfloat16
F32 = jnp.float32
TRANS = (((1,), (1,)), ((), ()))
FAR_FIRST = (4, 3, 5, 2, 6, 1, 7)


def dot(a, b):
    return jnp.dot(a, b, preferred_element_type=F32)


def dot_t(a, b):
    return lax.dot_general(a, b, TRANS, preferred_element_type=F32)


def kernel(x_in, g_in, st_in, fx_in, fg_in, up_in, dn_in, pk0_in, pk1_in, sc_in, cmp0_in, cmp1_in, exp_in,
           out_ref, dx_ref,
           shout, land, upf, dnf, upc, sendy0, ybuf0, sendy1, ybuf1, zbuf0, zbuf1, zsave, pp, xsend, xrecv,
           pbuf, ra, rb, rsend, ret,
           w_ss, w_rs, y_ss, y_rs, za_ss, za_rs, zb_ss, zb_rs, va_ss, va_rs, vb_ss, vb_rs, e_ss, e_rs,
           ra_ss, ra_rs, rb_ss, rb_rs, t_ss, t_rs, s_ss, s_rs):
    sec = lax.axis_index("section")
    me = lax.axis_index("expert")
    y = me // NZ
    z = me % NZ
    par = y % 2
    mate = (y + 1 - 2 * par) * NZ + z
    flip = sec % 2
    sgn = 1 - 2 * flip
    to_a = y * NZ + (z + sgn + NZ) % NZ
    to_b = y * NZ + (z - sgn + NZ) % NZ
    sec_up = (sec + 1) % 8
    sec_dn = (sec + 7) % 8

    def at(block):
        return (block + 2 * NZ) % NZ

    def remote(src, dst, ss, rs, expert, section=None):
        return pltpu.make_async_remote_copy(
            src_ref=src, dst_ref=dst, send_sem=ss, recv_sem=rs,
            device_id=(sec if section is None else section, expert),
            device_id_type=pl.DeviceIdType.MESH)

    barrier = pltpu.get_barrier_semaphore()
    peers = [(sec, ((y + k) % NY) * NZ + z) for k in range(1, NY)]
    peers += [(sec, to_a), (sec, to_b), (sec_up, me), (sec_dn, me)]
    for peer in peers:
        pl.semaphore_signal(barrier, inc=1, device_id=peer, device_id_type=pl.DeviceIdType.MESH)

    def cols(half, c):
        return slice(half * W + c * C, half * W + (c + 1) * C)

    def own_rows(t, which, half, c):
        if t == 0:
            return (x_in, g_in)[which][:, cols(half, c)]
        return land[which, c, half]

    def pick(t, c):
        for half in range(2):
            here = cols(half, c)
            if t == 0:
                terms = (x_in[:, here], st_in[0, :, here], g_in[:, here], st_in[1, :, here])
                pk, pad, buf = pk0_in, PAD, sendy0
            else:
                terms = (land[0, c, half], land[1, c, half])
                pk, pad, buf = pk1_in, 8, sendy1
            picked = dot(pk[0], terms[0])
            for s in range(1, len(terms)):
                picked = picked + dot(pk[s], terms[s])
            picked = picked.astype(BF)
            for e in range(WINDOW):
                buf[2 * e + half, c] = picked[e * pad:(e + 1) * pad]

    def across(buf, got, ss, rs, t, c):
        copies = []
        for k in FAR_FIRST:
            to = (y + k) % NY
            copies.append(remote(buf.at[to, c], got.at[y, c], ss.at[t, c, k], rs.at[t, c, k], to * NZ + z))
        return copies

    def weight_copies():
        away = pl.ds(pl.multiple_of((1 - par) * W, 128), W)
        return (
            remote(up_in.at[1 - par], upf.at[par], w_ss.at[0], w_rs.at[0], mate),
            remote(dn_in.at[:, away], dnf.at[par], w_ss.at[1], w_rs.at[1], mate),
        )

    def shift_copies(c):
        return (
            remote(shout.at[0, c], land.at[0, c], s_ss.at[0, c], s_rs.at[0, c], me, sec_up),
            remote(shout.at[1, c], land.at[1, c], s_ss.at[1, c], s_rs.at[1, c], me, sec_dn),
        )

    def save_a(h):
        b = at(z - sgn * h)
        return remote(zsave.at[b], zsave.at[b], va_ss.at[h], va_rs.at[h], to_a)

    def save_b(h):
        b = at(z + sgn * h)
        return remote(zsave.at[b], zsave.at[b], vb_ss.at[h], vb_rs.at[h], to_b)

    def save_hop(h):
        save_a(h).wait_recv()
        if h < 3:
            save_a(h + 1).start()
            save_b(h).wait_recv()
            if h < 2:
                save_b(h + 1).start()

    for c in range(2):
        pick(0, c)
    pl.semaphore_wait(barrier, len(peers))

    started = []
    for t in range(STEPS):
        buf, got = ((sendy0, ybuf0), (sendy1, ybuf1))[t]
        zbuf = (zbuf0, zbuf1)[t]
        sent_y = []
        for c in range(2):
            if t == 1:
                for copy in shift_copies(c):
                    copy.wait_recv()

                @pl.when(sec == 0)
                def _():
                    for half in range(2):
                        land[0, c, half] = fx_in[:, cols(half, c)]

                @pl.when(sec == 7)
                def _():
                    for half in range(2):
                        land[1, c, half] = fg_in[:, cols(half, c)]

                pick(1, c)
            sent = across(buf, got, y_ss, y_rs, t, c)
            for copy in sent:
                copy.start()
            got[y, c] = buf[y, c]
            sent_y.append(sent)
        if t == 1:
            save_hop(2)

        def go_a(h, c):
            b = at(z - sgn * h)
            return remote(zbuf.at[b, c], zbuf.at[b, c], za_ss.at[t, h, c], za_rs.at[t, h, c], to_a)

        def go_b(h, c):
            b = at(z + sgn * h)
            return remote(zbuf.at[b, c], zbuf.at[b, c], zb_ss.at[t, h, c], zb_rs.at[t, h, c], to_b)

        def swap(b):
            return remote(xsend.at[t, b], xrecv.at[t, b], e_ss.at[t, b], e_rs.at[t, b], mate)

        for c in range(2):
            for copy in sent_y[c]:
                copy.wait_recv()
            if t == 0:
                gathered = dot(cmp0_in[...], got[:, c].reshape(NY * PAD, C)).astype(BF)
                zbuf[z, c] = gathered[:ROWS]
                zsave[z, :, c * C:(c + 1) * C] = gathered[ROWS:]
            else:
                stacked = got[:, c].astype(F32).reshape(NY * 8, C).astype(BF)
                zbuf[z, c] = dot(cmp1_in[...], stacked).astype(BF)
            go_a(0, c).start()
            go_b(0, c).start()
        if t == 0:
            for copy in weight_copies():
                copy.start()

            @pl.when(par == 0)
            def _():
                upf[0] = up_in[0]
                dnf[0] = dn_in[:, :W]

            @pl.when(par == 1)
            def _():
                upf[1] = up_in[1]
                dnf[1] = dn_in[:, W:]
        else:
            save_hop(3)

        def first_half(b):
            rows = [zbuf[b, c] for c in range(2)]
            if t == 0:
                pre = dot(rows[0][:BACK], upc[:C]) + dot(rows[1][:BACK], upc[C:])
                grads = [r[BACK:] for r in rows]
            else:
                wide = [r.astype(F32) for r in rows]
                ahead = [w[:HALF].astype(BF) for w in wide]
                grads = [w[HALF:].astype(BF) for w in wide]
                pre = jnp.concatenate([
                    dot(ahead[0], upc[:C]) + dot(ahead[1], upc[C:]),
                    dot(zsave[b], upc[...])], axis=0)
            down = dnf[...].reshape(2 * HID_DEV, W)
            dh = dot_t(grads[0], down[:, :C]) + dot_t(grads[1], down[:, C:])
            both = jnp.concatenate([pre, dh], axis=0)
            pp[t, b] = both
            xsend[t, b] = both.astype(BF)
            swap(b).start()

        if t == 1:
            first_half(z)
        for h in range(4):
            for c in range(2):
                go_a(h, c).wait_recv()
                if h < 3:
                    go_a(h + 1, c).start()
                    go_b(h, c).wait_recv()
                    if h < 2:
                        go_b(h + 1, c).start()
            fresh = [h]
            if t == 0:
                fresh = [[], [], [0, 1, 2], [3]][h]
                if h == 2:
                    for copy in weight_copies():
                        copy.wait()
                    upc[:, :HID_DEV] = upf[0]
                    upc[:, HID_DEV:] = upf[1]
                    first_half(z)
            for k in fresh:
                first_half(at(z - sgn * (k + 1)))
                if k < 3:
                    first_half(at(z + sgn * (k + 1)))

        def second_half(b):
            swap(b).wait_recv()
            both = pp[t, b] + xrecv[t, b].astype(F32)
            v = both[:HALF]
            hidden = (v / (1.0 + jnp.exp(-v))).astype(BF)
            u = both[HALF:BACK]
            sigma = 1.0 / (1.0 + jnp.exp(-u))
            dpre = (both[BACK:] * (sigma * (1.0 + u * (1.0 - sigma)))).astype(BF)
            part = dot(hidden, dnf[...].reshape(2 * HID_DEV, W))
            for c in range(2):
                dpart = dot_t(dpre, upc[c * C:(c + 1) * C])
                pbuf[t, b, c] = jnp.concatenate([part[:, c * C:(c + 1) * C], dpart], axis=0).astype(BF)

        def back_a(h, c):
            b = at(z + sgn * (4 - h))
            return remote(pbuf.at[t, b, c], ra.at[t, h, c], ra_ss.at[t, h, c], ra_rs.at[t, h, c], to_a)

        def back_b(h, c):
            b = at(z - sgn * (3 - h))
            return remote(pbuf.at[t, b, c], rb.at[t, h, c], rb_ss.at[t, h, c], rb_rs.at[t, h, c], to_b)

        for h in range(4):
            a = at(z + sgn * (4 - h))
            b = at(z - sgn * (3 - h))
            second_half(a)
            if h == 0:
                for c in range(2):
                    back_a(0, c).start()
            second_half(b)
            if h == 0:
                for c in range(2):
                    back_b(0, c).start()
                continue
            for c in range(2):
                back_a(h - 1, c).wait_recv()
                pbuf[t, a, c] = (pbuf[t, a, c].astype(F32) + ra[t, h - 1, c].astype(F32)).astype(BF)
                back_a(h, c).start()
                if h < 3:
                    back_b(h - 1, c).wait_recv()
                    pbuf[t, b, c] = (pbuf[t, b, c].astype(F32) + rb[t, h - 1, c].astype(F32)).astype(BF)
                    back_b(h, c).start()
        if t == 0:
            save_a(0).start()
            save_b(0).start()
        sent_t = []
        for c in range(2):
            back_b(2, c).wait_recv()
            back_a(3, c).wait_recv()
            total = (pbuf[t, z, c].astype(F32) + ra[t, 3, c].astype(F32) + rb[t, 2, c].astype(F32)).astype(BF)
            spread = dot(exp_in[...], total).astype(BF)
            for k in range(NY):
                rsend[t, k, c] = spread[k * 8:(k + 1) * 8]
            sent = across(rsend.at[t], ret.at[t], t_ss, t_rs, t, c)
            for copy in sent:
                copy.start()
            ret[t, y, c] = rsend[t, y, c]
            sent_t.append(sent)
        if t == 0:
            save_hop(0)
        for c in range(2):
            for copy in sent_t[c]:
                copy.wait_recv()
            for half in range(2):
                totals = jnp.concatenate([ret[t, 2 * e + half, c].astype(F32) for e in range(WINDOW)], axis=0)
                for which in range(2):
                    mixed = jnp.dot(sc_in[t, which], totals, precision=lax.Precision.HIGHEST,
                                    preferred_element_type=F32)
                    value = (own_rows(t, which, half, c).astype(F32) + mixed).astype(BF)
                    if t == 0:
                        shout[which, c, half] = value
                    else:
                        (out_ref, dx_ref)[which][:, cols(half, c)] = value
            if t == 0:
                for copy in shift_copies(c):
                    copy.start()
        if t == 0:
            save_hop(1)

        for c in range(2):
            started += sent_y[c] + sent_t[c]
            for h in range(4):
                started += [go_a(h, c), back_a(h, c)]
            for h in range(3):
                started += [go_b(h, c), back_b(h, c)]
            if t == 0:
                started += list(shift_copies(c))
        started += [swap(b) for b in range(NZ)]
    started += [save_a(h) for h in range(4)] + [save_b(h) for h in range(3)]
    for copy in started:
        copy.wait_send()


def slot_plan(routes, gates):
    match = routes[..., None] == jnp.arange(WINDOW, dtype=jnp.int32)
    chosen = jnp.sum(match.astype(F32), axis=2)
    weight = jnp.sum(jnp.where(match, gates[..., None], 0.0), axis=2)
    ranks = jnp.cumsum(chosen, axis=1) - chosen
    places = (ranks[..., None] == jnp.arange(CAP, dtype=F32)).astype(F32)
    return places * chosen[..., None], weight


def plans(fr, fg, br, bg):
    pf, wf = slot_plan(fr, fg)
    pb, wb = slot_plan(br, bg)

    def picker(places, s, pad):
        m = jnp.transpose(places, (1, 2, 0))
        m = jnp.pad(m, ((0, 0), (s * CAP, pad - (s + 1) * CAP), (0, 0)))
        return m.reshape(WINDOW * pad, TOK).astype(BF)

    def scaler(places, weight, s):
        m = places * weight[..., None]
        m = jnp.pad(m, ((0, 0), (0, 0), (0, 0), (s * CAP, 8 - (s + 1) * CAP)))
        return m.reshape(STEPS, TOK, WINDOW * 8)

    pick0 = jnp.stack([picker(p, s, PAD) for s, p in enumerate((pf[0], pb[0], pb[0], pb[1]))])
    pick1 = jnp.stack([picker(p, s, 8) for s, p in enumerate((pf[1], pb[1]))])
    scale = jnp.stack([scaler(pf, wf, 0), scaler(pb, wb, 1)], axis=1)
    return pick0, pick1, scale


def row_map(streams, pad, forward):
    i = np.arange(streams * HALF)
    j = np.arange(NY * pad)
    s, k, c = i // HALF, (i % HALF) // CAP, i % CAP
    hit = (k * pad + s * CAP + c)[:, None] == j[None, :]
    return jnp.asarray(hit if forward else hit.T, BF)


def local(activations, gradients, stashed, fresh_activations, fresh_gradients, w_up, w_down,
          forward_routes, forward_gates, backward_routes, backward_gates):
    pick0, pick1, scale = plans(forward_routes[:, 0], forward_gates[:, 0], backward_routes[:, 0], backward_gates[:, 0])
    up = w_up[0].reshape(2, W, HID_DEV)
    vmem = pl.BlockSpec(memory_space=pltpu.VMEM)
    dma = pltpu.SemaphoreType.DMA
    shape = jax.ShapeDtypeStruct((TOK, D), BF)
    S = STEPS
    out, dx = pl.pallas_call(
        kernel,
        out_shape=(shape, shape),
        in_specs=[vmem] * 13,
        out_specs=(vmem, vmem),
        scratch_shapes=[
            pltpu.VMEM((2, 2, 2, TOK, C), BF),
            pltpu.VMEM((2, 2, 2, TOK, C), BF),
            pltpu.VMEM((2, W, HID_DEV), BF),
            pltpu.VMEM((2, HID_DEV, W), BF),
            pltpu.VMEM((W, 2 * HID_DEV), BF),
            pltpu.VMEM((NY, 2, PAD, C), BF),
            pltpu.VMEM((NY, 2, PAD, C), BF),
            pltpu.VMEM((NY, 2, 8, C), BF),
            pltpu.VMEM((NY, 2, 8, C), BF),
            pltpu.VMEM((NZ, 2, ROWS, C), BF),
            pltpu.VMEM((NZ, 2, BACK, C), BF),
            pltpu.VMEM((NZ, HALF, W), BF),
            pltpu.VMEM((S, NZ, ROWS, 2 * HID_DEV), F32),
            pltpu.VMEM((S, NZ, ROWS, 2 * HID_DEV), BF),
            pltpu.VMEM((S, NZ, ROWS, 2 * HID_DEV), BF),
            pltpu.VMEM((S, NZ, 2, BACK, C), BF),
            pltpu.VMEM((S, 4, 2, BACK, C), BF),
            pltpu.VMEM((S, 3, 2, BACK, C), BF),
            pltpu.VMEM((S, NY, 2, 8, C), BF),
            pltpu.VMEM((S, NY, 2, 8, C), BF),
            dma((2,)), dma((2,)),
            dma((S, 2, NY)), dma((S, 2, NY)),
            dma((S, 4, 2)), dma((S, 4, 2)),
            dma((S, 3, 2)), dma((S, 3, 2)),
            dma((4,)), dma((4,)),
            dma((3,)), dma((3,)),
            dma((S, NZ)), dma((S, NZ)),
            dma((S, 4, 2)), dma((S, 4, 2)),
            dma((S, 3, 2)), dma((S, 3, 2)),
            dma((S, 2, NY)), dma((S, 2, NY)),
            dma((2, 2)), dma((2, 2)),
        ],
        compiler_params=pltpu.CompilerParams(
            collective_id=0, has_side_effects=True, vmem_limit_bytes=60 * 1024 * 1024),
    )(activations[0], gradients[0], stashed[:, 0], fresh_activations[0], fresh_gradients[0],
      up, w_down[0], pick0, pick1, scale, row_map(4, PAD, True), row_map(2, 8, True), row_map(2, 8, False))
    return out[None], dx[None]


def solution(mesh):
    placed = (
        P("section", "expert", None),
        P("section", "expert", None),
        P(None, "section", "expert", None),
        P(None, "expert", None),
        P(None, "expert", None),
        P("section", None, "expert"),
        P("section", "expert", None),
        P(None, "section", "expert", None),
        P(None, "section", "expert", None),
        P(None, "section", "expert", None),
        P(None, "section", "expert", None),
    )
    return jax.shard_map(
        local,
        mesh=mesh,
        in_specs=placed,
        out_specs=(P("section", "expert", None), P("section", "expert", None)),
        check_vma=False,
    )
```

```python
import jax
import jax.numpy as jnp
import numpy as np
from jax import lax
from jax.experimental import pallas as pl
from jax.experimental.pallas import tpu as pltpu
from jax.sharding import PartitionSpec as P

CAP = 3
STEPS = 2
WINDOW = 4
TOK = 64
D = 3584
W = D // 2
C = W // 2
HID_DEV = 128
NY = 8
NZ = 8
PAD = 16
ROWS = 3 * NY * CAP
BACK = 2 * NY * CAP
HALF = NY * CAP
BF = jnp.bfloat16
F32 = jnp.float32
TRANS = (((1,), (1,)), ((), ()))
FAR_FIRST = (4, 3, 5, 2, 6, 1, 7)


def dot(a, b):
    return jnp.dot(a, b, preferred_element_type=F32)


def dot_t(a, b):
    return lax.dot_general(a, b, TRANS, preferred_element_type=F32)


def kernel(x_in, g_in, st_in, fx_in, fg_in, up_in, dn_in, fr_in, fg_w, br_in, bg_w, cmp0_in, cmp1_in, exp_in,
           out_ref, dx_ref,
           shout, land, upf, dnf, upc, sendy0, ybuf0, sendy1, ybuf1, zbuf0, zbuf1, zsave, pp, xsend, xrecv,
           pbuf, ra, rb, rsend, ret,
           w_ss, w_rs, y_ss, y_rs, za_ss, za_rs, zb_ss, zb_rs, va_ss, va_rs, vb_ss, vb_rs, e_ss, e_rs,
           ra_ss, ra_rs, rb_ss, rb_rs, t_ss, t_rs, s_ss, s_rs, d_ss, d_rs,
           dsend, drecv, pk0, pk1, scales):
    sec = lax.axis_index("section")
    me = lax.axis_index("expert")
    y = me // NZ
    z = me % NZ
    par = y % 2
    mate = (y + 1 - 2 * par) * NZ + z
    flip = sec % 2
    sgn = 1 - 2 * flip
    to_a = y * NZ + (z + sgn + NZ) % NZ
    to_b = y * NZ + (z - sgn + NZ) % NZ
    sec_up = (sec + 1) % 8
    sec_dn = (sec + 7) % 8

    def at(block):
        return (block + 2 * NZ) % NZ

    def remote(src, dst, ss, rs, expert, section=None):
        return pltpu.make_async_remote_copy(
            src_ref=src, dst_ref=dst, send_sem=ss, recv_sem=rs,
            device_id=(sec if section is None else section, expert),
            device_id_type=pl.DeviceIdType.MESH)

    barrier = pltpu.get_barrier_semaphore()
    peers = [(sec, ((y + k) % NY) * NZ + z) for k in range(1, NY)]
    peers += [(sec, to_a), (sec, to_b), (sec_up, me), (sec_dn, me)]
    for peer in peers:
        pl.semaphore_signal(barrier, inc=1, device_id=peer, device_id_type=pl.DeviceIdType.MESH)

    def cols(half, c):
        return slice(half * W + c * C, half * W + (c + 1) * C)

    def own_rows(t, which, half, c):
        if t == 0:
            return (x_in, g_in)[which][:, cols(half, c)]
        return land[which, c, half]

    def pick(t, c):
        for half in range(2):
            here = cols(half, c)
            if t == 0:
                terms = (x_in[:, here], st_in[0, :, here], g_in[:, here], st_in[1, :, here])
                pk, pad, buf = pk0, PAD, sendy0
            else:
                terms = (land[0, c, half], land[1, c, half])
                pk, pad, buf = pk1, 8, sendy1
            picked = dot(pk[0], terms[0])
            for s in range(1, len(terms)):
                picked = picked + dot(pk[s], terms[s])
            picked = picked.astype(BF)
            for e in range(WINDOW):
                buf[2 * e + half, c] = picked[e * pad:(e + 1) * pad]

    def across(buf, got, ss, rs, t, c):
        copies = []
        for k in FAR_FIRST:
            to = (y + k) % NY
            copies.append(remote(buf.at[to, c], got.at[y, c], ss.at[t, c, k], rs.at[t, c, k], to * NZ + z))
        return copies

    def weight_copies():
        away = pl.ds(pl.multiple_of((1 - par) * W, 128), W)
        return (
            remote(up_in.at[1 - par], upf.at[par], w_ss.at[0], w_rs.at[0], mate),
            remote(dn_in.at[:, away], dnf.at[par], w_ss.at[1], w_rs.at[1], mate),
        )

    def shift_copies(c):
        return (
            remote(shout.at[0, c], land.at[0, c], s_ss.at[0, c], s_rs.at[0, c], me, sec_up),
            remote(shout.at[1, c], land.at[1, c], s_ss.at[1, c], s_rs.at[1, c], me, sec_dn),
        )

    def save_a(h):
        b = at(z - sgn * h)
        return remote(zsave.at[b], zsave.at[b], va_ss.at[h], va_rs.at[h], to_a)

    def save_b(h):
        b = at(z + sgn * h)
        return remote(zsave.at[b], zsave.at[b], vb_ss.at[h], vb_rs.at[h], to_b)

    def save_hop(h):
        save_a(h).wait_recv()
        if h < 3:
            save_a(h + 1).start()
            save_b(h).wait_recv()
            if h < 2:
                save_b(h + 1).start()

    earlier = (lax.broadcasted_iota(jnp.int32, (TOK, TOK), 1)
               < lax.broadcasted_iota(jnp.int32, (TOK, TOK), 0)).astype(F32).astype(BF)
    wide = lax.broadcasted_iota(jnp.int32, (TOK, WINDOW * PAD), 1)
    thin = lax.broadcasted_iota(jnp.int32, (TOK, WINDOW * 8), 1)
    for t in range(STEPS):
        for which, (routes, gates) in enumerate(((fr_in, fg_w), (br_in, bg_w))):
            ids, weights = routes[t], gates[t]
            named, weight = [], []
            for e in range(WINDOW):
                match = ids == e
                named.append(jnp.sum(jnp.where(match, 1.0, 0.0), axis=1, keepdims=True))
                weight.append(jnp.sum(jnp.where(match, weights, 0.0), axis=1, keepdims=True))
            scaled = jnp.zeros((TOK, WINDOW * 8), F32)
            places = [jnp.zeros((TOK, WINDOW * PAD), F32) for s in range(4)]
            short = jnp.zeros((TOK, WINDOW * 8), F32)
            for e in range(WINDOW):
                rank = dot(earlier, jnp.broadcast_to(named[e], (TOK, 128)).astype(BF))[:, :1]
                for c in range(CAP):
                    here = jnp.where(rank == float(c), named[e], 0.0)
                    scaled = scaled + jnp.where(thin == e * 8 + which * CAP + c, here * weight[e], 0.0)
                    short = short + jnp.where(thin == e * 8 + which * CAP + c, here, 0.0)
                    for s in range(4):
                        places[s] = places[s] + jnp.where(wide == e * PAD + s * CAP + c, here, 0.0)
            high = scaled.astype(BF)
            left = scaled - high.astype(F32)
            mid = left.astype(BF)
            low = (left - mid.astype(F32)).astype(BF)
            scales[t, which, 0] = high
            scales[t, which, 1] = mid
            scales[t, which, 2] = low
            if t == 0:
                for s in ((0,), (1, 2))[which]:
                    pk0[s] = places[s].T.astype(BF)
            else:
                pk1[which] = short.T.astype(BF)
                if which == 1:
                    pk0[3] = places[3].T.astype(BF)

    for c in range(2):
        pick(0, c)
    pl.semaphore_wait(barrier, len(peers))

    started = []
    for t in range(STEPS):
        buf, got = ((sendy0, ybuf0), (sendy1, ybuf1))[t]
        zbuf = (zbuf0, zbuf1)[t]
        sent_y = []
        for c in range(2):
            if t == 1:
                for copy in shift_copies(c):
                    copy.wait_recv()

                @pl.when(sec == 0)
                def _():
                    for half in range(2):
                        land[0, c, half] = fx_in[:, cols(half, c)]

                @pl.when(sec == 7)
                def _():
                    for half in range(2):
                        land[1, c, half] = fg_in[:, cols(half, c)]

                pick(1, c)
            sent = across(buf, got, y_ss, y_rs, t, c)
            for copy in sent:
                copy.start()
            got[y, c] = buf[y, c]
            sent_y.append(sent)
        if t == 1:
            save_hop(2)

        def go_a(h, c):
            b = at(z - sgn * h)
            return remote(zbuf.at[b, c], zbuf.at[b, c], za_ss.at[t, h, c], za_rs.at[t, h, c], to_a)

        def go_b(h, c):
            b = at(z + sgn * h)
            return remote(zbuf.at[b, c], zbuf.at[b, c], zb_ss.at[t, h, c], zb_rs.at[t, h, c], to_b)

        def swap(b):
            return remote(xsend.at[t, b], xrecv.at[t, b], e_ss.at[t, b], e_rs.at[t, b], mate)

        def swap_d(b):
            return remote(dsend.at[t, b], drecv.at[t, b], d_ss.at[t, b], d_rs.at[t, b], mate)

        for c in range(2):
            for copy in sent_y[c]:
                copy.wait_recv()
            if t == 0:
                gathered = dot(cmp0_in[...], got[:, c].reshape(NY * PAD, C)).astype(BF)
                zbuf[z, c] = gathered[:ROWS]
                zsave[z, :, c * C:(c + 1) * C] = gathered[ROWS:]
            else:
                stacked = got[:, c].astype(F32).reshape(NY * 8, C).astype(BF)
                zbuf[z, c] = dot(cmp1_in[...], stacked).astype(BF)
            go_a(0, c).start()
            go_b(0, c).start()
            if t == 0 and c == 0:
                for copy in weight_copies():
                    copy.start()
        if t == 0:
            @pl.when(par == 0)
            def _():
                upf[0] = up_in[0]
                dnf[0] = dn_in[:, :W]

            @pl.when(par == 1)
            def _():
                upf[1] = up_in[1]
                dnf[1] = dn_in[:, W:]
        else:
            save_hop(3)

        def pre_half(b):
            rows = [zbuf[b, c] for c in range(2)]
            if t == 0:
                pre = dot(rows[0][:BACK], upc[:C]) + dot(rows[1][:BACK], upc[C:])
            else:
                ahead = [r.astype(F32)[:HALF].astype(BF) for r in rows]
                pre = jnp.concatenate([
                    dot(ahead[0], upc[:C]) + dot(ahead[1], upc[C:]),
                    dot(zsave[b], upc[...])], axis=0)
            pp[t, b, :BACK] = pre
            xsend[t, b] = pre.astype(BF)
            swap(b).start()

        def grad_half(b):
            rows = [zbuf[b, c] for c in range(2)]
            if t == 0:
                grads = [r[BACK:] for r in rows]
            else:
                grads = [r.astype(F32)[HALF:].astype(BF) for r in rows]
            down = dnf[...].reshape(2 * HID_DEV, W)
            dh = dot_t(grads[0], down[:, :C]) + dot_t(grads[1], down[:, C:])
            pp[t, b, BACK:] = dh
            dsend[t, b] = dh.astype(BF)
            swap_d(b).start()

        def landed(k):
            return [at(z - sgn * (k + 1))] + ([at(z + sgn * (k + 1))] if k < 3 else [])

        if t == 1:
            pre_half(z)
            grad_half(z)
        for h in range(4):
            for c in range(2):
                go_a(h, c).wait_recv()
                if h < 3:
                    go_a(h + 1, c).start()
                    go_b(h, c).wait_recv()
                    if h < 2:
                        go_b(h + 1, c).start()
            if t == 0 and h == 1:
                weight_copies()[0].wait()
                upc[:, :HID_DEV] = upf[0]
                upc[:, HID_DEV:] = upf[1]
                for b in [z] + landed(0):
                    pre_half(b)
            if t == 1 or h >= 1:
                for b in landed(h):
                    pre_half(b)
            if t == 0 and h == 2:
                weight_copies()[1].wait()
                for b in [z] + landed(0) + landed(1):
                    grad_half(b)
            if t == 1 or h >= 2:
                for b in landed(h):
                    grad_half(b)

        def second_half(b):
            swap(b).wait_recv()
            both = pp[t, b, :BACK] + xrecv[t, b].astype(F32)
            v = both[:HALF]
            hidden = (v / (1.0 + jnp.exp(-v))).astype(BF)
            u = both[HALF:BACK]
            sigma = 1.0 / (1.0 + jnp.exp(-u))
            swap_d(b).wait_recv()
            slope_in = pp[t, b, BACK:] + drecv[t, b].astype(F32)
            dpre = (slope_in * (sigma * (1.0 + u * (1.0 - sigma)))).astype(BF)
            part = dot(hidden, dnf[...].reshape(2 * HID_DEV, W))
            for c in range(2):
                dpart = dot_t(dpre, upc[c * C:(c + 1) * C])
                pbuf[t, b, c] = jnp.concatenate([part[:, c * C:(c + 1) * C], dpart], axis=0).astype(BF)

        def back_a(h, c):
            b = at(z + sgn * (4 - h))
            return remote(pbuf.at[t, b, c], ra.at[t, h, c], ra_ss.at[t, h, c], ra_rs.at[t, h, c], to_a)

        def back_b(h, c):
            b = at(z - sgn * (3 - h))
            return remote(pbuf.at[t, b, c], rb.at[t, h, c], rb_ss.at[t, h, c], rb_rs.at[t, h, c], to_b)

        for h in range(4):
            a = at(z + sgn * (4 - h))
            b = at(z - sgn * (3 - h))
            second_half(a)
            if h == 0:
                for c in range(2):
                    back_a(0, c).start()
            second_half(b)
            if h == 0:
                for c in range(2):
                    back_b(0, c).start()
                continue
            for c in range(2):
                back_a(h - 1, c).wait_recv()
                pbuf[t, a, c] = (pbuf[t, a, c].astype(F32) + ra[t, h - 1, c].astype(F32)).astype(BF)
                back_a(h, c).start()
                if h < 3:
                    back_b(h - 1, c).wait_recv()
                    pbuf[t, b, c] = (pbuf[t, b, c].astype(F32) + rb[t, h - 1, c].astype(F32)).astype(BF)
                    back_b(h, c).start()
        if t == 0:
            save_a(0).start()
            save_b(0).start()
        sent_t = []
        for c in range(2):
            back_b(2, c).wait_recv()
            back_a(3, c).wait_recv()
            total = (pbuf[t, z, c].astype(F32) + ra[t, 3, c].astype(F32) + rb[t, 2, c].astype(F32)).astype(BF)
            spread = dot(exp_in[...], total).astype(BF)
            for k in range(NY):
                rsend[t, k, c] = spread[k * 8:(k + 1) * 8]
            sent = across(rsend.at[t], ret.at[t], t_ss, t_rs, t, c)
            for copy in sent:
                copy.start()
            ret[t, y, c] = rsend[t, y, c]
            sent_t.append(sent)
        if t == 0:
            save_hop(0)
        for c in range(2):
            for copy in sent_t[c]:
                copy.wait_recv()
            for half in range(2):
                totals = jnp.concatenate([ret[t, 2 * e + half, c].astype(F32) for e in range(WINDOW)], axis=0).astype(BF)
                for which in range(2):
                    mixed = (dot(scales[t, which, 2], totals) + dot(scales[t, which, 1], totals)
                             + dot(scales[t, which, 0], totals))
                    value = (own_rows(t, which, half, c).astype(F32) + mixed).astype(BF)
                    if t == 0:
                        shout[which, c, half] = value
                    else:
                        (out_ref, dx_ref)[which][:, cols(half, c)] = value
            if t == 0:
                for copy in shift_copies(c):
                    copy.start()
        if t == 0:
            save_hop(1)

        for c in range(2):
            started += sent_y[c] + sent_t[c]
            for h in range(4):
                started += [go_a(h, c), back_a(h, c)]
            for h in range(3):
                started += [go_b(h, c), back_b(h, c)]
            if t == 0:
                started += list(shift_copies(c))
        started += [swap(b) for b in range(NZ)] + [swap_d(b) for b in range(NZ)]
    started += [save_a(h) for h in range(4)] + [save_b(h) for h in range(3)]
    for copy in started:
        copy.wait_send()


def row_map(streams, pad, forward):
    i = np.arange(streams * HALF)
    j = np.arange(NY * pad)
    s, k, c = i // HALF, (i % HALF) // CAP, i % CAP
    hit = (k * pad + s * CAP + c)[:, None] == j[None, :]
    return jnp.asarray(hit if forward else hit.T, BF)


def local(activations, gradients, stashed, fresh_activations, fresh_gradients, w_up, w_down,
          forward_routes, forward_gates, backward_routes, backward_gates):
    up = w_up[0].reshape(2, W, HID_DEV)
    vmem = pl.BlockSpec(memory_space=pltpu.VMEM)
    dma = pltpu.SemaphoreType.DMA
    shape = jax.ShapeDtypeStruct((TOK, D), BF)
    S = STEPS
    out, dx = pl.pallas_call(
        kernel,
        out_shape=(shape, shape),
        in_specs=[vmem] * 14,
        out_specs=(vmem, vmem),
        scratch_shapes=[
            pltpu.VMEM((2, 2, 2, TOK, C), BF),
            pltpu.VMEM((2, 2, 2, TOK, C), BF),
            pltpu.VMEM((2, W, HID_DEV), BF),
            pltpu.VMEM((2, HID_DEV, W), BF),
            pltpu.VMEM((W, 2 * HID_DEV), BF),
            pltpu.VMEM((NY, 2, PAD, C), BF),
            pltpu.VMEM((NY, 2, PAD, C), BF),
            pltpu.VMEM((NY, 2, 8, C), BF),
            pltpu.VMEM((NY, 2, 8, C), BF),
            pltpu.VMEM((NZ, 2, ROWS, C), BF),
            pltpu.VMEM((NZ, 2, BACK, C), BF),
            pltpu.VMEM((NZ, HALF, W), BF),
            pltpu.VMEM((S, NZ, ROWS, 2 * HID_DEV), F32),
            pltpu.VMEM((S, NZ, BACK, 2 * HID_DEV), BF),
            pltpu.VMEM((S, NZ, BACK, 2 * HID_DEV), BF),
            pltpu.VMEM((S, NZ, 2, BACK, C), BF),
            pltpu.VMEM((S, 4, 2, BACK, C), BF),
            pltpu.VMEM((S, 3, 2, BACK, C), BF),
            pltpu.VMEM((S, NY, 2, 8, C), BF),
            pltpu.VMEM((S, NY, 2, 8, C), BF),
            dma((2,)), dma((2,)),
            dma((S, 2, NY)), dma((S, 2, NY)),
            dma((S, 4, 2)), dma((S, 4, 2)),
            dma((S, 3, 2)), dma((S, 3, 2)),
            dma((4,)), dma((4,)),
            dma((3,)), dma((3,)),
            dma((S, NZ)), dma((S, NZ)),
            dma((S, 4, 2)), dma((S, 4, 2)),
            dma((S, 3, 2)), dma((S, 3, 2)),
            dma((S, 2, NY)), dma((S, 2, NY)),
            dma((2, 2)), dma((2, 2)),
            dma((S, NZ)), dma((S, NZ)),
            pltpu.VMEM((S, NZ, HALF, 2 * HID_DEV), BF),
            pltpu.VMEM((S, NZ, HALF, 2 * HID_DEV), BF),
            pltpu.VMEM((4, WINDOW * PAD, TOK), BF),
            pltpu.VMEM((2, WINDOW * 8, TOK), BF),
            pltpu.VMEM((S, 2, 3, TOK, WINDOW * 8), BF),
        ],
        compiler_params=pltpu.CompilerParams(
            collective_id=0, has_side_effects=True, vmem_limit_bytes=60 * 1024 * 1024),
    )(activations[0], gradients[0], stashed[:, 0], fresh_activations[0], fresh_gradients[0],
      up, w_down[0], forward_routes[:, 0], forward_gates[:, 0],
      backward_routes[:, 0], backward_gates[:, 0],
      row_map(4, PAD, True), row_map(2, 8, True), row_map(2, 8, False))
    return out[None], dx[None]


def solution(mesh):
    placed = (
        P("section", "expert", None),
        P("section", "expert", None),
        P(None, "section", "expert", None),
        P(None, "expert", None),
        P(None, "expert", None),
        P("section", None, "expert"),
        P("section", "expert", None),
        P(None, "section", "expert", None),
        P(None, "section", "expert", None),
        P(None, "section", "expert", None),
        P(None, "section", "expert", None),
    )
    return jax.shard_map(
        local,
        mesh=mesh,
        in_specs=placed,
        out_specs=(P("section", "expert", None), P("section", "expert", None)),
        check_vma=False,
    )
```

```python
import jax
import jax.numpy as jnp
import numpy as np
from jax import lax
from jax.experimental import pallas as pl
from jax.experimental.pallas import tpu as pltpu
from jax.sharding import PartitionSpec as P

CAP = 3
STEPS = 2
WINDOW = 4
TOK = 64
D = 3584
W = D // 2
C = W // 2
HID_DEV = 128
NY = 8
NZ = 8
PAD = 16
ROWS = 3 * NY * CAP
BACK = 2 * NY * CAP
HALF = NY * CAP
BF = jnp.bfloat16
F32 = jnp.float32
TRANS = (((1,), (1,)), ((), ()))
FAR_FIRST = (4, 3, 5, 2, 6, 1, 7)


def dot(a, b):
    return jnp.dot(a, b, preferred_element_type=F32)


def dot_t(a, b):
    return lax.dot_general(a, b, TRANS, preferred_element_type=F32)


def kernel(x_in, g_in, st_in, fx_in, fg_in, up_in, dn_in, fr_in, fg_w, br_in, bg_w, cmp0_in, cmp1_in, exp_in,
           out_ref, dx_ref,
           shout, land, upf, dnf, upc, sendy0, ybuf0, sendy1, ybuf1, zbuf0, zbuf1, zsave, pp, xsend, xrecv,
           pbuf, ra, rb, rsend, ret,
           w_ss, w_rs, y_ss, y_rs, za_ss, za_rs, zb_ss, zb_rs, va_ss, va_rs, vb_ss, vb_rs, e_ss, e_rs,
           ra_ss, ra_rs, rb_ss, rb_rs, t_ss, t_rs, s_ss, s_rs, d_ss, d_rs,
           dsend, drecv, pk0, pk1, scales, l_sem):
    sec = lax.axis_index("section")
    me = lax.axis_index("expert")
    y = me // NZ
    z = me % NZ
    par = y % 2
    mate = (y + 1 - 2 * par) * NZ + z
    flip = sec % 2
    sgn = 1 - 2 * flip
    to_a = y * NZ + (z + sgn + NZ) % NZ
    to_b = y * NZ + (z - sgn + NZ) % NZ
    sec_up = (sec + 1) % 8
    sec_dn = (sec + 7) % 8

    def at(block):
        return (block + 2 * NZ) % NZ

    def remote(src, dst, ss, rs, expert, section=None):
        return pltpu.make_async_remote_copy(
            src_ref=src, dst_ref=dst, send_sem=ss, recv_sem=rs,
            device_id=(sec if section is None else section, expert),
            device_id_type=pl.DeviceIdType.MESH)

    barrier = pltpu.get_barrier_semaphore()
    peers = [(sec, ((y + k) % NY) * NZ + z) for k in range(1, NY)]
    peers += [(sec, to_a), (sec, to_b), (sec_up, me), (sec_dn, me)]
    for peer in peers:
        pl.semaphore_signal(barrier, inc=1, device_id=peer, device_id_type=pl.DeviceIdType.MESH)

    def cols(half, c):
        return slice(half * W + c * C, half * W + (c + 1) * C)

    def own_rows(t, which, half, c):
        if t == 0:
            return (x_in, g_in)[which][:, cols(half, c)]
        return land[which, c, half]

    def pick(t, c):
        for half in range(2):
            here = cols(half, c)
            if t == 0:
                terms = (x_in[:, here], st_in[0, :, here], g_in[:, here], st_in[1, :, here])
                pk, pad, buf = pk0, PAD, sendy0
            else:
                terms = (land[0, c, half], land[1, c, half])
                pk, pad, buf = pk1, 8, sendy1
            picked = dot(pk[0], terms[0])
            for s in range(1, len(terms)):
                picked = picked + dot(pk[s], terms[s])
            picked = picked.astype(BF)
            for e in range(WINDOW):
                buf[2 * e + half, c] = picked[e * pad:(e + 1) * pad]

    def across(buf, got, ss, rs, t, c):
        copies = []
        for k in FAR_FIRST:
            to = (y + k) % NY
            copies.append(remote(buf.at[to, c], got.at[y, c], ss.at[t, c, k], rs.at[t, c, k], to * NZ + z))
        return copies

    def weight_copies():
        away = pl.ds(pl.multiple_of((1 - par) * W, 128), W)
        return (
            remote(up_in.at[1 - par], upf.at[par], w_ss.at[0], w_rs.at[0], mate),
            remote(dn_in.at[:, away], dnf.at[par], w_ss.at[1], w_rs.at[1], mate),
        )

    def own_weights():
        mine = pl.ds(pl.multiple_of(par * W, 128), W)
        return (
            pltpu.make_async_copy(up_in.at[par], upf.at[par], l_sem.at[0]),
            pltpu.make_async_copy(dn_in.at[:, mine], dnf.at[par], l_sem.at[1]),
        )

    def shift_copies(c):
        return (
            remote(shout.at[0, c], land.at[0, c], s_ss.at[0, c], s_rs.at[0, c], me, sec_up),
            remote(shout.at[1, c], land.at[1, c], s_ss.at[1, c], s_rs.at[1, c], me, sec_dn),
        )

    def save_a(h):
        b = at(z - sgn * h)
        return remote(zsave.at[b], zsave.at[b], va_ss.at[h], va_rs.at[h], to_a)

    def save_b(h):
        b = at(z + sgn * h)
        return remote(zsave.at[b], zsave.at[b], vb_ss.at[h], vb_rs.at[h], to_b)

    def save_hop(h):
        save_a(h).wait_recv()
        if h < 3:
            save_a(h + 1).start()
            save_b(h).wait_recv()
            if h < 2:
                save_b(h + 1).start()

    for copy in own_weights():
        copy.start()
    earlier = (lax.broadcasted_iota(jnp.int32, (TOK, TOK), 0)
               < lax.broadcasted_iota(jnp.int32, (TOK, TOK), 1)).astype(F32).astype(BF)
    wide = lax.broadcasted_iota(jnp.int32, (WINDOW * PAD, TOK), 0)
    thin = lax.broadcasted_iota(jnp.int32, (WINDOW * 8, TOK), 0)
    for t in range(STEPS):
        for which, (routes, gates) in enumerate(((fr_in, fg_w), (br_in, bg_w))):
            ids, weights = routes[t], gates[t]
            named, weight = [], []
            for e in range(WINDOW):
                match = ids == e
                named.append(jnp.sum(jnp.where(match, 1.0, 0.0), axis=0, keepdims=True))
                weight.append(jnp.sum(jnp.where(match, weights, 0.0), axis=0, keepdims=True))
            scaled = jnp.zeros((WINDOW * 8, TOK), F32)
            places = [jnp.zeros((WINDOW * PAD, TOK), F32) for s in range(4)]
            short = jnp.zeros((WINDOW * 8, TOK), F32)
            for e in range(WINDOW):
                rank = dot(jnp.broadcast_to(named[e], (16, TOK)).astype(BF), earlier)[:1]
                for c in range(CAP):
                    here = jnp.where(rank == float(c), named[e], 0.0)
                    scaled = scaled + jnp.where(thin == e * 8 + which * CAP + c, here * weight[e], 0.0)
                    short = short + jnp.where(thin == e * 8 + which * CAP + c, here, 0.0)
                    for s in range(4):
                        places[s] = places[s] + jnp.where(wide == e * PAD + s * CAP + c, here, 0.0)
            scaled = scaled.T
            high = scaled.astype(BF)
            left = scaled - high.astype(F32)
            mid = left.astype(BF)
            low = (left - mid.astype(F32)).astype(BF)
            scales[t, which, 0] = high
            scales[t, which, 1] = mid
            scales[t, which, 2] = low
            if t == 0:
                for s in ((0,), (1, 2))[which]:
                    pk0[s] = places[s].astype(BF)
            else:
                pk1[which] = short.astype(BF)
                if which == 1:
                    pk0[3] = places[3].astype(BF)

    for c in range(2):
        pick(0, c)
    pl.semaphore_wait(barrier, len(peers))

    started = []
    for t in range(STEPS):
        buf, got = ((sendy0, ybuf0), (sendy1, ybuf1))[t]
        zbuf = (zbuf0, zbuf1)[t]
        sent_y = []
        for c in range(2):
            if t == 1:
                for copy in shift_copies(c):
                    copy.wait_recv()

                @pl.when(sec == 0)
                def _():
                    for half in range(2):
                        land[0, c, half] = fx_in[:, cols(half, c)]

                @pl.when(sec == 7)
                def _():
                    for half in range(2):
                        land[1, c, half] = fg_in[:, cols(half, c)]

                pick(1, c)
            sent = across(buf, got, y_ss, y_rs, t, c)
            for copy in sent:
                copy.start()
            got[y, c] = buf[y, c]
            sent_y.append(sent)
        if t == 1:
            save_hop(2)

        def go_a(h, c):
            b = at(z - sgn * h)
            return remote(zbuf.at[b, c], zbuf.at[b, c], za_ss.at[t, h, c], za_rs.at[t, h, c], to_a)

        def go_b(h, c):
            b = at(z + sgn * h)
            return remote(zbuf.at[b, c], zbuf.at[b, c], zb_ss.at[t, h, c], zb_rs.at[t, h, c], to_b)

        def swap(b):
            return remote(xsend.at[t, b], xrecv.at[t, b], e_ss.at[t, b], e_rs.at[t, b], mate)

        def swap_d(b):
            return remote(dsend.at[t, b], drecv.at[t, b], d_ss.at[t, b], d_rs.at[t, b], mate)

        for c in range(2):
            for copy in sent_y[c]:
                copy.wait_recv()
            if t == 0:
                gathered = dot(cmp0_in[...], got[:, c].reshape(NY * PAD, C)).astype(BF)
                zbuf[z, c] = gathered[:ROWS]
                zsave[z, :, c * C:(c + 1) * C] = gathered[ROWS:]
            else:
                stacked = got[:, c].astype(F32).reshape(NY * 8, C).astype(BF)
                zbuf[z, c] = dot(cmp1_in[...], stacked).astype(BF)
            go_a(0, c).start()
            go_b(0, c).start()
            if t == 0 and c == 0:
                for copy in weight_copies():
                    copy.start()
        if t == 1:
            save_hop(3)

        def pre_half(b):
            rows = [zbuf[b, c] for c in range(2)]
            if t == 0:
                pre = dot(rows[0][:BACK], upc[:C]) + dot(rows[1][:BACK], upc[C:])
            else:
                ahead = [r.astype(F32)[:HALF].astype(BF) for r in rows]
                pre = jnp.concatenate([
                    dot(ahead[0], upc[:C]) + dot(ahead[1], upc[C:]),
                    dot(zsave[b], upc[...])], axis=0)
            pp[t, b, :BACK] = pre
            xsend[t, b] = pre.astype(BF)
            swap(b).start()

        def grad_half(b):
            rows = [zbuf[b, c] for c in range(2)]
            if t == 0:
                grads = [r[BACK:] for r in rows]
            else:
                grads = [r.astype(F32)[HALF:].astype(BF) for r in rows]
            down = dnf[...].reshape(2 * HID_DEV, W)
            dh = dot_t(grads[0], down[:, :C]) + dot_t(grads[1], down[:, C:])
            pp[t, b, BACK:] = dh
            dsend[t, b] = dh.astype(BF)
            swap_d(b).start()

        def landed(k):
            return [at(z - sgn * (k + 1))] + ([at(z + sgn * (k + 1))] if k < 3 else [])

        def second_half(b):
            swap(b).wait_recv()
            both = pp[t, b, :BACK] + xrecv[t, b].astype(F32)
            v = both[:HALF]
            hidden = (v / (1.0 + jnp.exp(-v))).astype(BF)
            u = both[HALF:BACK]
            sigma = 1.0 / (1.0 + jnp.exp(-u))
            swap_d(b).wait_recv()
            slope_in = pp[t, b, BACK:] + drecv[t, b].astype(F32)
            dpre = (slope_in * (sigma * (1.0 + u * (1.0 - sigma)))).astype(BF)
            part = dot(hidden, dnf[...].reshape(2 * HID_DEV, W))
            for c in range(2):
                dpart = dot_t(dpre, upc[c * C:(c + 1) * C])
                pbuf[t, b, c] = jnp.concatenate([part[:, c * C:(c + 1) * C], dpart], axis=0).astype(BF)

        def back_a(h, c):
            b = at(z + sgn * (4 - h))
            return remote(pbuf.at[t, b, c], ra.at[t, h, c], ra_ss.at[t, h, c], ra_rs.at[t, h, c], to_a)

        def back_b(h, c):
            b = at(z - sgn * (3 - h))
            return remote(pbuf.at[t, b, c], rb.at[t, h, c], rb_ss.at[t, h, c], rb_rs.at[t, h, c], to_b)

        if t == 1:
            pre_half(z)
            grad_half(z)
        for h in range(4):
            for c in range(2):
                go_a(h, c).wait_recv()
                if h < 3:
                    go_a(h + 1, c).start()
                    go_b(h, c).wait_recv()
                    if h < 2:
                        go_b(h + 1, c).start()
            if t == 0 and h == 1:
                weight_copies()[0].wait()
                own_weights()[0].wait()
                upc[:, :HID_DEV] = upf[0]
                upc[:, HID_DEV:] = upf[1]
                for b in [z] + landed(0):
                    pre_half(b)
            if t == 1 or h >= 1:
                for b in landed(h):
                    pre_half(b)
            if t == 0 and h == 2:
                weight_copies()[1].wait()
                own_weights()[1].wait()
                for b in [z] + landed(0) + landed(1):
                    grad_half(b)
            if t == 1 or h >= 2:
                for b in landed(h):
                    grad_half(b)
            if h == 2:
                first_b = at(z - sgn * 3)
                second_half(first_b)
                for c in range(2):
                    back_b(0, c).start()

        for h in range(4):
            a = at(z + sgn * (4 - h))
            b = at(z - sgn * (3 - h))
            second_half(a)
            if h == 0:
                for c in range(2):
                    back_a(0, c).start()
                continue
            second_half(b)
            for c in range(2):
                back_a(h - 1, c).wait_recv()
                pbuf[t, a, c] = (pbuf[t, a, c].astype(F32) + ra[t, h - 1, c].astype(F32)).astype(BF)
                back_a(h, c).start()
                if h < 3:
                    back_b(h - 1, c).wait_recv()
                    pbuf[t, b, c] = (pbuf[t, b, c].astype(F32) + rb[t, h - 1, c].astype(F32)).astype(BF)
                    back_b(h, c).start()
        if t == 0:
            save_a(0).start()
            save_b(0).start()
        sent_t = []
        for c in range(2):
            back_b(2, c).wait_recv()
            back_a(3, c).wait_recv()
            total = (pbuf[t, z, c].astype(F32) + ra[t, 3, c].astype(F32) + rb[t, 2, c].astype(F32)).astype(BF)
            spread = dot(exp_in[...], total).astype(BF)
            for k in range(NY):
                rsend[t, k, c] = spread[k * 8:(k + 1) * 8]
            sent = across(rsend.at[t], ret.at[t], t_ss, t_rs, t, c)
            for copy in sent:
                copy.start()
            ret[t, y, c] = rsend[t, y, c]
            sent_t.append(sent)
        if t == 0:
            save_hop(0)
        for c in range(2):
            for copy in sent_t[c]:
                copy.wait_recv()
            for half in range(2):
                totals = jnp.concatenate([ret[t, 2 * e + half, c].astype(F32) for e in range(WINDOW)], axis=0).astype(BF)
                for which in range(2):
                    mixed = (dot(scales[t, which, 2], totals) + dot(scales[t, which, 1], totals)
                             + dot(scales[t, which, 0], totals))
                    value = (own_rows(t, which, half, c).astype(F32) + mixed).astype(BF)
                    if t == 0:
                        shout[which, c, half] = value
                    else:
                        (out_ref, dx_ref)[which][:, cols(half, c)] = value
            if t == 0:
                for copy in shift_copies(c):
                    copy.start()
        if t == 0:
            save_hop(1)

        for c in range(2):
            started += sent_y[c] + sent_t[c]
            for h in range(4):
                started += [go_a(h, c), back_a(h, c)]
            for h in range(3):
                started += [go_b(h, c), back_b(h, c)]
            if t == 0:
                started += list(shift_copies(c))
        started += [swap(b) for b in range(NZ)] + [swap_d(b) for b in range(NZ)]
    started += [save_a(h) for h in range(4)] + [save_b(h) for h in range(3)]
    for copy in started:
        copy.wait_send()


def row_map(streams, pad, forward):
    i = np.arange(streams * HALF)
    j = np.arange(NY * pad)
    s, k, c = i // HALF, (i % HALF) // CAP, i % CAP
    hit = (k * pad + s * CAP + c)[:, None] == j[None, :]
    return jnp.asarray(hit if forward else hit.T, BF)


def local(activations, gradients, stashed, fresh_activations, fresh_gradients, w_up, w_down,
          forward_routes, forward_gates, backward_routes, backward_gates):
    up = w_up[0].reshape(2, W, HID_DEV)
    vmem = pl.BlockSpec(memory_space=pltpu.VMEM)
    dma = pltpu.SemaphoreType.DMA
    shape = jax.ShapeDtypeStruct((TOK, D), BF)
    S = STEPS
    out, dx = pl.pallas_call(
        kernel,
        out_shape=(shape, shape),
        in_specs=[vmem] * 5 + [pl.BlockSpec(memory_space=pl.ANY)] * 2 + [vmem] * 7,
        out_specs=(vmem, vmem),
        scratch_shapes=[
            pltpu.VMEM((2, 2, 2, TOK, C), BF),
            pltpu.VMEM((2, 2, 2, TOK, C), BF),
            pltpu.VMEM((2, W, HID_DEV), BF),
            pltpu.VMEM((2, HID_DEV, W), BF),
            pltpu.VMEM((W, 2 * HID_DEV), BF),
            pltpu.VMEM((NY, 2, PAD, C), BF),
            pltpu.VMEM((NY, 2, PAD, C), BF),
            pltpu.VMEM((NY, 2, 8, C), BF),
            pltpu.VMEM((NY, 2, 8, C), BF),
            pltpu.VMEM((NZ, 2, ROWS, C), BF),
            pltpu.VMEM((NZ, 2, BACK, C), BF),
            pltpu.VMEM((NZ, HALF, W), BF),
            pltpu.VMEM((S, NZ, ROWS, 2 * HID_DEV), F32),
            pltpu.VMEM((S, NZ, BACK, 2 * HID_DEV), BF),
            pltpu.VMEM((S, NZ, BACK, 2 * HID_DEV), BF),
            pltpu.VMEM((S, NZ, 2, BACK, C), BF),
            pltpu.VMEM((S, 4, 2, BACK, C), BF),
            pltpu.VMEM((S, 3, 2, BACK, C), BF),
            pltpu.VMEM((S, NY, 2, 8, C), BF),
            pltpu.VMEM((S, NY, 2, 8, C), BF),
            dma((2,)), dma((2,)),
            dma((S, 2, NY)), dma((S, 2, NY)),
            dma((S, 4, 2)), dma((S, 4, 2)),
            dma((S, 3, 2)), dma((S, 3, 2)),
            dma((4,)), dma((4,)),
            dma((3,)), dma((3,)),
            dma((S, NZ)), dma((S, NZ)),
            dma((S, 4, 2)), dma((S, 4, 2)),
            dma((S, 3, 2)), dma((S, 3, 2)),
            dma((S, 2, NY)), dma((S, 2, NY)),
            dma((2, 2)), dma((2, 2)),
            dma((S, NZ)), dma((S, NZ)),
            pltpu.VMEM((S, NZ, HALF, 2 * HID_DEV), BF),
            pltpu.VMEM((S, NZ, HALF, 2 * HID_DEV), BF),
            pltpu.VMEM((4, WINDOW * PAD, TOK), BF),
            pltpu.VMEM((2, WINDOW * 8, TOK), BF),
            pltpu.VMEM((S, 2, 3, TOK, WINDOW * 8), BF),
            dma((2,)),
        ],
        compiler_params=pltpu.CompilerParams(
            collective_id=0, has_side_effects=True, vmem_limit_bytes=60 * 1024 * 1024),
    )(activations[0], gradients[0], stashed[:, 0], fresh_activations[0], fresh_gradients[0],
      up, w_down[0], jnp.swapaxes(forward_routes[:, 0], 1, 2), jnp.swapaxes(forward_gates[:, 0], 1, 2),
      jnp.swapaxes(backward_routes[:, 0], 1, 2), jnp.swapaxes(backward_gates[:, 0], 1, 2),
      row_map(4, PAD, True), row_map(2, 8, True), row_map(2, 8, False))
    return out[None], dx[None]


def solution(mesh):
    placed = (
        P("section", "expert", None),
        P("section", "expert", None),
        P(None, "section", "expert", None),
        P(None, "expert", None),
        P(None, "expert", None),
        P("section", None, "expert"),
        P("section", "expert", None),
        P(None, "section", "expert", None),
        P(None, "section", "expert", None),
        P(None, "section", "expert", None),
        P(None, "section", "expert", None),
    )
    return jax.shard_map(
        local,
        mesh=mesh,
        in_specs=placed,
        out_specs=(P("section", "expert", None), P("section", "expert", None)),
        check_vma=False,
    )
```

```python
import jax
import jax.numpy as jnp
import numpy as np
from jax import lax
from jax.experimental import pallas as pl
from jax.experimental.pallas import tpu as pltpu
from jax.sharding import PartitionSpec as P

CAP = 3
STEPS = 2
WINDOW = 4
TOK = 64
D = 3584
W = D // 2
C = W // 2
HID_DEV = 128
NY = 8
NZ = 8
PAD = 16
ROWS = 3 * NY * CAP
BACK = 2 * NY * CAP
HALF = NY * CAP
BF = jnp.bfloat16
F32 = jnp.float32
TRANS = (((1,), (1,)), ((), ()))
FAR_FIRST = (4, 3, 5, 2, 6, 1, 7)


def dot(a, b):
    return jnp.dot(a, b, preferred_element_type=F32)


def dot_t(a, b):
    return lax.dot_general(a, b, TRANS, preferred_element_type=F32)


def kernel(x_in, g_in, st_in, fx_in, fg_in, up_in, dn_in, fr_in, fg_w, br_in, bg_w, cmp0_in, cmp1_in, exp_in,
           out_ref, dx_ref,
           shout, land, upf, dnf, upc, sendy0, ybuf0, sendy1, ybuf1, zbuf0, zbuf1, zsave, pp, xsend, xrecv,
           pbuf, ra, rb, rsend, ret,
           w_ss, w_rs, y_ss, y_rs, za_ss, za_rs, zb_ss, zb_rs, va_ss, va_rs, vb_ss, vb_rs, e_ss, e_rs,
           ra_ss, ra_rs, rb_ss, rb_rs, t_ss, t_rs, s_ss, s_rs, d_ss, d_rs,
           dsend, drecv, pk0, pk1, scales):
    sec = lax.axis_index("section")
    me = lax.axis_index("expert")
    y = me // NZ
    z = me % NZ
    par = y % 2
    mate = (y + 1 - 2 * par) * NZ + z
    flip = sec % 2
    sgn = 1 - 2 * flip
    to_a = y * NZ + (z + sgn + NZ) % NZ
    to_b = y * NZ + (z - sgn + NZ) % NZ
    sec_up = (sec + 1) % 8
    sec_dn = (sec + 7) % 8

    def at(block):
        return (block + 2 * NZ) % NZ

    def remote(src, dst, ss, rs, expert, section=None):
        return pltpu.make_async_remote_copy(
            src_ref=src, dst_ref=dst, send_sem=ss, recv_sem=rs,
            device_id=(sec if section is None else section, expert),
            device_id_type=pl.DeviceIdType.MESH)

    barrier = pltpu.get_barrier_semaphore()
    peers = [(sec, ((y + k) % NY) * NZ + z) for k in range(1, NY)]
    peers += [(sec, to_a), (sec, to_b), (sec_up, me), (sec_dn, me)]
    for peer in peers:
        pl.semaphore_signal(barrier, inc=1, device_id=peer, device_id_type=pl.DeviceIdType.MESH)

    def cols(half, c):
        return slice(half * W + c * C, half * W + (c + 1) * C)

    def own_rows(t, which, half, c):
        if t == 0:
            return (x_in, g_in)[which][:, cols(half, c)]
        return land[which, c, half]

    def pick(t, c):
        for half in range(2):
            here = cols(half, c)
            if t == 0:
                terms = (x_in[:, here], st_in[0, :, here], g_in[:, here], st_in[1, :, here])
                pk, pad, buf = pk0, PAD, sendy0
            else:
                terms = (land[0, c, half], land[1, c, half])
                pk, pad, buf = pk1, 8, sendy1
            picked = dot(pk[0], terms[0])
            for s in range(1, len(terms)):
                picked = picked + dot(pk[s], terms[s])
            picked = picked.astype(BF)
            for e in range(WINDOW):
                buf[2 * e + half, c] = picked[e * pad:(e + 1) * pad]

    def across(buf, got, ss, rs, t, c):
        copies = []
        for k in FAR_FIRST:
            to = (y + k) % NY
            copies.append(remote(buf.at[to, c], got.at[y, c], ss.at[t, c, k], rs.at[t, c, k], to * NZ + z))
        return copies

    def weight_copies():
        away = pl.ds(pl.multiple_of((1 - par) * W, 128), W)
        return (
            remote(up_in.at[1 - par], upf.at[par], w_ss.at[0], w_rs.at[0], mate),
            remote(dn_in.at[:, away], dnf.at[par], w_ss.at[1], w_rs.at[1], mate),
        )

    def shift_copies(c):
        return (
            remote(shout.at[0, c], land.at[0, c], s_ss.at[0, c], s_rs.at[0, c], me, sec_up),
            remote(shout.at[1, c], land.at[1, c], s_ss.at[1, c], s_rs.at[1, c], me, sec_dn),
        )

    def save_a(h):
        b = at(z - sgn * h)
        return remote(zsave.at[b], zsave.at[b], va_ss.at[h], va_rs.at[h], to_a)

    def save_b(h):
        b = at(z + sgn * h)
        return remote(zsave.at[b], zsave.at[b], vb_ss.at[h], vb_rs.at[h], to_b)

    def save_hop(h):
        save_a(h).wait_recv()
        if h < 3:
            save_a(h + 1).start()
            save_b(h).wait_recv()
            if h < 2:
                save_b(h + 1).start()

    earlier = (lax.broadcasted_iota(jnp.int32, (TOK, TOK), 0)
               < lax.broadcasted_iota(jnp.int32, (TOK, TOK), 1)).astype(F32).astype(BF)
    wide = lax.broadcasted_iota(jnp.int32, (WINDOW * PAD, TOK), 0)
    thin = lax.broadcasted_iota(jnp.int32, (WINDOW * 8, TOK), 0)
    for t in range(STEPS):
        for which, (routes, gates) in enumerate(((fr_in, fg_w), (br_in, bg_w))):
            ids, weights = routes[t], gates[t]
            named, weight = [], []
            for e in range(WINDOW):
                match = ids == e
                named.append(jnp.sum(jnp.where(match, 1.0, 0.0), axis=0, keepdims=True))
                weight.append(jnp.sum(jnp.where(match, weights, 0.0), axis=0, keepdims=True))
            scaled = jnp.zeros((WINDOW * 8, TOK), F32)
            places = [jnp.zeros((WINDOW * PAD, TOK), F32) for s in range(4)]
            short = jnp.zeros((WINDOW * 8, TOK), F32)
            for e in range(WINDOW):
                rank = dot(jnp.broadcast_to(named[e], (16, TOK)).astype(BF), earlier)[:1]
                for c in range(CAP):
                    here = jnp.where(rank == float(c), named[e], 0.0)
                    scaled = scaled + jnp.where(thin == e * 8 + which * CAP + c, here * weight[e], 0.0)
                    short = short + jnp.where(thin == e * 8 + which * CAP + c, here, 0.0)
                    for s in range(4):
                        places[s] = places[s] + jnp.where(wide == e * PAD + s * CAP + c, here, 0.0)
            scaled = scaled.T
            high = scaled.astype(BF)
            left = scaled - high.astype(F32)
            mid = left.astype(BF)
            low = (left - mid.astype(F32)).astype(BF)
            scales[t, which, 0] = high
            scales[t, which, 1] = mid
            scales[t, which, 2] = low
            if t == 0:
                for s in ((0,), (1, 2))[which]:
                    pk0[s] = places[s].astype(BF)
            else:
                pk1[which] = short.astype(BF)
                if which == 1:
                    pk0[3] = places[3].astype(BF)

    for c in range(2):
        pick(0, c)
    pl.semaphore_wait(barrier, len(peers))

    started = []
    for t in range(STEPS):
        buf, got = ((sendy0, ybuf0), (sendy1, ybuf1))[t]
        zbuf = (zbuf0, zbuf1)[t]
        sent_y = []
        for c in range(2):
            if t == 1:
                for copy in shift_copies(c):
                    copy.wait_recv()

                @pl.when(sec == 0)
                def _():
                    for half in range(2):
                        land[0, c, half] = fx_in[:, cols(half, c)]

                @pl.when(sec == 7)
                def _():
                    for half in range(2):
                        land[1, c, half] = fg_in[:, cols(half, c)]

                pick(1, c)
            sent = across(buf, got, y_ss, y_rs, t, c)
            for copy in sent:
                copy.start()
            got[y, c] = buf[y, c]
            sent_y.append(sent)
        if t == 1:
            save_hop(2)

        def go_a(h, c):
            b = at(z - sgn * h)
            return remote(zbuf.at[b, c], zbuf.at[b, c], za_ss.at[t, h, c], za_rs.at[t, h, c], to_a)

        def go_b(h, c):
            b = at(z + sgn * h)
            return remote(zbuf.at[b, c], zbuf.at[b, c], zb_ss.at[t, h, c], zb_rs.at[t, h, c], to_b)

        def swap(b):
            return remote(xsend.at[t, b], xrecv.at[t, b], e_ss.at[t, b], e_rs.at[t, b], mate)

        def swap_d(b):
            return remote(dsend.at[t, b], drecv.at[t, b], d_ss.at[t, b], d_rs.at[t, b], mate)

        for c in range(2):
            for copy in sent_y[c]:
                copy.wait_recv()
            if t == 0:
                gathered = dot(cmp0_in[...], got[:, c].reshape(NY * PAD, C)).astype(BF)
                zbuf[z, c] = gathered[:ROWS]
                zsave[z, :, c * C:(c + 1) * C] = gathered[ROWS:]
            else:
                stacked = got[:, c].astype(F32).reshape(NY * 8, C).astype(BF)
                zbuf[z, c] = dot(cmp1_in[...], stacked).astype(BF)
            go_a(0, c).start()
            go_b(0, c).start()
            if t == 0 and c == 0:
                for copy in weight_copies():
                    copy.start()
        if t == 0:
            @pl.when(par == 0)
            def _():
                upf[0] = up_in[0]
                dnf[0] = dn_in[:, :W]

            @pl.when(par == 1)
            def _():
                upf[1] = up_in[1]
                dnf[1] = dn_in[:, W:]
        else:
            save_hop(3)

        def pre_half(b):
            rows = [zbuf[b, c] for c in range(2)]
            if t == 0:
                pre = dot(rows[0][:BACK], upc[:C]) + dot(rows[1][:BACK], upc[C:])
            else:
                ahead = [r.astype(F32)[:HALF].astype(BF) for r in rows]
                pre = jnp.concatenate([
                    dot(ahead[0], upc[:C]) + dot(ahead[1], upc[C:]),
                    dot(zsave[b], upc[...])], axis=0)
            pp[t, b, :BACK] = pre
            xsend[t, b] = pre.astype(BF)
            swap(b).start()

        def grad_half(b):
            rows = [zbuf[b, c] for c in range(2)]
            if t == 0:
                grads = [r[BACK:] for r in rows]
            else:
                grads = [r.astype(F32)[HALF:].astype(BF) for r in rows]
            down = dnf[...].reshape(2 * HID_DEV, W)
            dh = dot_t(grads[0], down[:, :C]) + dot_t(grads[1], down[:, C:])
            pp[t, b, BACK:] = dh
            dsend[t, b] = dh.astype(BF)
            swap_d(b).start()

        def landed(k):
            return [at(z - sgn * (k + 1))] + ([at(z + sgn * (k + 1))] if k < 3 else [])

        def second_half(b):
            swap(b).wait_recv()
            both = pp[t, b, :BACK] + xrecv[t, b].astype(F32)
            v = both[:HALF]
            hidden = (v / (1.0 + jnp.exp(-v))).astype(BF)
            u = both[HALF:BACK]
            sigma = 1.0 / (1.0 + jnp.exp(-u))
            swap_d(b).wait_recv()
            slope_in = pp[t, b, BACK:] + drecv[t, b].astype(F32)
            dpre = (slope_in * (sigma * (1.0 + u * (1.0 - sigma)))).astype(BF)
            part = dot(hidden, dnf[...].reshape(2 * HID_DEV, W))
            for c in range(2):
                dpart = dot_t(dpre, upc[c * C:(c + 1) * C])
                pbuf[t, b, c] = jnp.concatenate([part[:, c * C:(c + 1) * C], dpart], axis=0).astype(BF)

        def back_a(h, c):
            b = at(z + sgn * (4 - h))
            return remote(pbuf.at[t, b, c], ra.at[t, h, c], ra_ss.at[t, h, c], ra_rs.at[t, h, c], to_a)

        def back_b(h, c):
            b = at(z - sgn * (3 - h))
            return remote(pbuf.at[t, b, c], rb.at[t, h, c], rb_ss.at[t, h, c], rb_rs.at[t, h, c], to_b)

        if t == 1:
            pre_half(z)
            grad_half(z)
        for h in range(4):
            for c in range(2):
                go_a(h, c).wait_recv()
                if h < 3:
                    go_a(h + 1, c).start()
                    go_b(h, c).wait_recv()
                    if h < 2:
                        go_b(h + 1, c).start()
            if t == 0 and h == 1:
                weight_copies()[0].wait()
                upc[:, :HID_DEV] = upf[0]
                upc[:, HID_DEV:] = upf[1]
                for b in [z] + landed(0):
                    pre_half(b)
            if t == 1 or h >= 1:
                for b in landed(h):
                    pre_half(b)
            if t == 0 and h == 2:
                weight_copies()[1].wait()
                for b in [z] + landed(0) + landed(1):
                    grad_half(b)
            if t == 1 or h >= 2:
                for b in landed(h):
                    grad_half(b)
            if h == 3:
                first_b = at(z - sgn * 3)
                second_half(first_b)
                for c in range(2):
                    back_b(0, c).start()

        for h in range(4):
            a = at(z + sgn * (4 - h))
            b = at(z - sgn * (3 - h))
            second_half(a)
            if h == 0:
                for c in range(2):
                    back_a(0, c).start()
                continue
            second_half(b)
            for c in range(2):
                back_a(h - 1, c).wait_recv()
                pbuf[t, a, c] = (pbuf[t, a, c].astype(F32) + ra[t, h - 1, c].astype(F32)).astype(BF)
                back_a(h, c).start()
                if h < 3:
                    back_b(h - 1, c).wait_recv()
                    pbuf[t, b, c] = (pbuf[t, b, c].astype(F32) + rb[t, h - 1, c].astype(F32)).astype(BF)
                    back_b(h, c).start()
        if t == 0:
            save_a(0).start()
            save_b(0).start()
        sent_t = []
        for c in range(2):
            back_b(2, c).wait_recv()
            back_a(3, c).wait_recv()
            total = (pbuf[t, z, c].astype(F32) + ra[t, 3, c].astype(F32) + rb[t, 2, c].astype(F32)).astype(BF)
            spread = dot(exp_in[...], total).astype(BF)
            for k in range(NY):
                rsend[t, k, c] = spread[k * 8:(k + 1) * 8]
            sent = across(rsend.at[t], ret.at[t], t_ss, t_rs, t, c)
            for copy in sent:
                copy.start()
            ret[t, y, c] = rsend[t, y, c]
            sent_t.append(sent)
        if t == 0:
            save_hop(0)
        for c in range(2):
            for copy in sent_t[c]:
                copy.wait_recv()
            for half in range(2):
                totals = jnp.concatenate([ret[t, 2 * e + half, c].astype(F32) for e in range(WINDOW)], axis=0).astype(BF)
                for which in range(2):
                    mixed = (dot(scales[t, which, 2], totals) + dot(scales[t, which, 1], totals)
                             + dot(scales[t, which, 0], totals))
                    value = (own_rows(t, which, half, c).astype(F32) + mixed).astype(BF)
                    if t == 0:
                        shout[which, c, half] = value
                    else:
                        (out_ref, dx_ref)[which][:, cols(half, c)] = value
            if t == 0:
                for copy in shift_copies(c):
                    copy.start()
        if t == 0:
            save_hop(1)

        for c in range(2):
            started += sent_y[c] + sent_t[c]
            for h in range(4):
                started += [go_a(h, c), back_a(h, c)]
            for h in range(3):
                started += [go_b(h, c), back_b(h, c)]
            if t == 0:
                started += list(shift_copies(c))
        started += [swap(b) for b in range(NZ)] + [swap_d(b) for b in range(NZ)]
    started += [save_a(h) for h in range(4)] + [save_b(h) for h in range(3)]
    for copy in started:
        copy.wait_send()


def row_map(streams, pad, forward):
    i = np.arange(streams * HALF)
    j = np.arange(NY * pad)
    s, k, c = i // HALF, (i % HALF) // CAP, i % CAP
    hit = (k * pad + s * CAP + c)[:, None] == j[None, :]
    return jnp.asarray(hit if forward else hit.T, BF)


def local(activations, gradients, stashed, fresh_activations, fresh_gradients, w_up, w_down,
          forward_routes, forward_gates, backward_routes, backward_gates):
    up = w_up[0].reshape(2, W, HID_DEV)
    vmem = pl.BlockSpec(memory_space=pltpu.VMEM)
    dma = pltpu.SemaphoreType.DMA
    shape = jax.ShapeDtypeStruct((TOK, D), BF)
    S = STEPS
    out, dx = pl.pallas_call(
        kernel,
        out_shape=(shape, shape),
        in_specs=[vmem] * 14,
        out_specs=(vmem, vmem),
        scratch_shapes=[
            pltpu.VMEM((2, 2, 2, TOK, C), BF),
            pltpu.VMEM((2, 2, 2, TOK, C), BF),
            pltpu.VMEM((2, W, HID_DEV), BF),
            pltpu.VMEM((2, HID_DEV, W), BF),
            pltpu.VMEM((W, 2 * HID_DEV), BF),
            pltpu.VMEM((NY, 2, PAD, C), BF),
            pltpu.VMEM((NY, 2, PAD, C), BF),
            pltpu.VMEM((NY, 2, 8, C), BF),
            pltpu.VMEM((NY, 2, 8, C), BF),
            pltpu.VMEM((NZ, 2, ROWS, C), BF),
            pltpu.VMEM((NZ, 2, BACK, C), BF),
            pltpu.VMEM((NZ, HALF, W), BF),
            pltpu.VMEM((S, NZ, ROWS, 2 * HID_DEV), F32),
            pltpu.VMEM((S, NZ, BACK, 2 * HID_DEV), BF),
            pltpu.VMEM((S, NZ, BACK, 2 * HID_DEV), BF),
            pltpu.VMEM((S, NZ, 2, BACK, C), BF),
            pltpu.VMEM((S, 4, 2, BACK, C), BF),
            pltpu.VMEM((S, 3, 2, BACK, C), BF),
            pltpu.VMEM((S, NY, 2, 8, C), BF),
            pltpu.VMEM((S, NY, 2, 8, C), BF),
            dma((2,)), dma((2,)),
            dma((S, 2, NY)), dma((S, 2, NY)),
            dma((S, 4, 2)), dma((S, 4, 2)),
            dma((S, 3, 2)), dma((S, 3, 2)),
            dma((4,)), dma((4,)),
            dma((3,)), dma((3,)),
            dma((S, NZ)), dma((S, NZ)),
            dma((S, 4, 2)), dma((S, 4, 2)),
            dma((S, 3, 2)), dma((S, 3, 2)),
            dma((S, 2, NY)), dma((S, 2, NY)),
            dma((2, 2)), dma((2, 2)),
            dma((S, NZ)), dma((S, NZ)),
            pltpu.VMEM((S, NZ, HALF, 2 * HID_DEV), BF),
            pltpu.VMEM((S, NZ, HALF, 2 * HID_DEV), BF),
            pltpu.VMEM((4, WINDOW * PAD, TOK), BF),
            pltpu.VMEM((2, WINDOW * 8, TOK), BF),
            pltpu.VMEM((S, 2, 3, TOK, WINDOW * 8), BF),
        ],
        compiler_params=pltpu.CompilerParams(
            collective_id=0, has_side_effects=True, vmem_limit_bytes=60 * 1024 * 1024),
    )(activations[0], gradients[0], stashed[:, 0], fresh_activations[0], fresh_gradients[0],
      up, w_down[0], jnp.swapaxes(forward_routes[:, 0], 1, 2), jnp.swapaxes(forward_gates[:, 0], 1, 2),
      jnp.swapaxes(backward_routes[:, 0], 1, 2), jnp.swapaxes(backward_gates[:, 0], 1, 2),
      row_map(4, PAD, True), row_map(2, 8, True), row_map(2, 8, False))
    return out[None], dx[None]


def solution(mesh):
    placed = (
        P("section", "expert", None),
        P("section", "expert", None),
        P(None, "section", "expert", None),
        P(None, "expert", None),
        P(None, "expert", None),
        P("section", None, "expert"),
        P("section", "expert", None),
        P(None, "section", "expert", None),
        P(None, "section", "expert", None),
        P(None, "section", "expert", None),
        P(None, "section", "expert", None),
    )
    return jax.shard_map(
        local,
        mesh=mesh,
        in_specs=placed,
        out_specs=(P("section", "expert", None), P("section", "expert", None)),
        check_vma=False,
    )
```
